256 devices in a mesh: dp: 32 (over z_lo, y, core), tensor: 8 (over z_hi, x).
Axes of the slice: x: 4, y: 4, z: 8 (z_hi: 2, z_lo: 4; z = z_hi * 4 + z_lo), core: 2. Of those that a mesh axis runs over, the one named last changes fastest.
Arguments:
- layer_inputs: bfloat16 [4096, 8192], P('dp', 'tensor'), may hold values from -6 to 6
- out_grads: bfloat16 [4096, 14336], P('dp', 'tensor'), may hold values from -0.09375 to 0.09375
- basis: float32 [8192, 512], P('tensor'), may hold values from -0.0625 to 0.0625
- first: float32 [512, 14336], P('dp', 'tensor'), may hold values from -3 to 3
- second: float32 [512, 14336], P('dp', 'tensor'), may hold values from 0.05 to 2
Outputs:
- new_basis: float32 [8192, 512], P('tensor')
- new_first: float32 [512, 14336], P('dp', 'tensor')
- new_second: float32 [512, 14336], P('dp', 'tensor')
- update: float32 [512, 14336], P('dp', 'tensor')
The draws below stay inside these ranges and needn't reach their ends.
All inputs are finite; a program needn't handle non-finite values.
Results may differ from the reference program's by a relative error of at most 0.0013.
The reference program's roundings to bfloat16 on the way (of `basis_low`, `scores`, `grad_low`, `backward`, `left_low` and `probe`) count: a program that leaves them out, or rounds other values in their place, can miss the bound.
Values may be sent and summed in bfloat16 or wider, within the bound.
No kernel may reach another device: no remote copies, remote signals or barrier semaphores. Data moves between devices by JAX's collectives and lax.ppermute only.
A program may use at most 64 MiB of HBM per device.

```python
import math
import jax
import jax.numpy as jnp
from jax import lax

D = 8192
FF = 14336
RANK = 512
PI_STEPS = 6
TOKENS = 4096


def levels(key, shape, cuts, low, top_value):
    def one(dim, blocks):
        heights = jax.random.uniform(jax.random.fold_in(jax.random.fold_in(key, 6), dim), (blocks,), jnp.float32, low / len(cuts), top_value / len(cuts))
        return jnp.repeat(jnp.exp(heights), shape[dim] // blocks).reshape((-1,) + (1,) * (len(shape) - dim - 1))

    gain = one(*cuts[0])
    for cut in cuts[1:]:
        gain = gain * one(*cut)
    return gain


def bell_draw(own_key, dims, scale, most, split=(), kind=jnp.bfloat16):
    entries = jax.random.normal(own_key, dims, jnp.float32) * scale
    if len(split) > 0:
        entries = levels(own_key, dims, split, -0.22, 0.18) * entries
    return jnp.clip(entries, min=-most, max=most).astype(kind)


def setup_inputs(seed: int = 0) -> dict:
    keys = jax.random.split(jax.random.key(seed), 6)
    return {
        "layer_inputs": bell_draw(keys[0], (TOKENS, D), 1.0, 6.0, ((0, 32), (1, 8))),
        "out_grads": bell_draw(keys[1], (TOKENS, FF), TOKENS ** -0.5, 0.09375, ((0, 32), (1, 8))),
        "basis": bell_draw(keys[2], (D, RANK), D ** -0.5, 0.0625, ((0, 8),), jnp.float32),
        "first": bell_draw(keys[3], (RANK, FF), 0.5, 3.0, ((0, 32), (1, 8)), jnp.float32),
        "second": jnp.clip(jnp.exp(math.log(2.0) - 3.6888794 * jax.random.uniform(keys[4], (RANK, FF), jnp.float32) ** levels(keys[4], (RANK, FF), ((0, 32), (1, 8)), -0.2, 0.2)), 0.05, 2.0),
    }


EXACT = lax.Precision.HIGHEST

def matmul(left, right):
    return jnp.dot(left, right, precision=EXACT, preferred_element_type=jnp.float32)

def leading(normed):
    rank_count = normed.shape[0]
    vector = jnp.ones((rank_count,), jnp.float32) / jnp.sqrt(jnp.float32(rank_count))
    for sweep in range(PI_STEPS):
        vector = matmul(normed, vector)
        vector = vector / jnp.sqrt(jnp.sum(vector * vector) + 1e-12)
    return vector

def reference(layer_inputs, out_grads, basis, first, second):
    basis_low = basis.astype(jnp.bfloat16)
    scores = jnp.dot(layer_inputs, basis_low, preferred_element_type=jnp.float32).astype(jnp.bfloat16)
    grad_proj = jnp.dot(scores.T, out_grads, preferred_element_type=jnp.float32)
    grad_low = grad_proj.astype(jnp.bfloat16)
    backward = jnp.dot(out_grads, grad_low.T, preferred_element_type=jnp.float32).astype(jnp.bfloat16)
    tangent = jnp.dot(layer_inputs.T, backward, preferred_element_type=jnp.float32)
    coupling = matmul(basis.T, tangent)
    resid = tangent - matmul(basis, coupling)
    kernel = matmul(resid.T, resid)
    total = jnp.trace(kernel)
    normed = kernel / total
    vector = leading(normed)
    ratio = jnp.sum(vector * matmul(normed, vector))
    theta = 4.0 * jnp.sqrt(ratio)
    sigma = jnp.sqrt(total * ratio + 1e-06)
    left_vec = matmul(resid, vector) / sigma
    cosine_val = jnp.cos(theta)
    sine_val = jnp.sin(theta)
    basis_dir = matmul(basis, vector)
    new_basis = basis + (cosine_val - 1.0) * jnp.outer(basis_dir, vector) + sine_val * jnp.outer(left_vec, vector)
    rotation = matmul(new_basis.T, basis)
    left_low = left_vec.astype(jnp.bfloat16)
    probe = jnp.dot(layer_inputs, left_low, preferred_element_type=jnp.float32).astype(jnp.bfloat16)
    along = jnp.dot(probe, out_grads, preferred_element_type=jnp.float32)
    lead_row = matmul(vector, grad_proj)
    grad_new = grad_proj + (cosine_val - 1.0) * jnp.outer(vector, lead_row) + sine_val * jnp.outer(vector, along)
    new_first = 0.9 * matmul(rotation, first) + 0.1 * grad_new
    new_second = 0.95 * matmul(rotation * rotation, second) + 0.05 * grad_new * grad_new
    update = new_first / (jnp.sqrt(new_second) + 1e-06)
    return (new_basis, new_first, new_second, update)
```

```python
import jax
import jax.numpy as jnp
from jax import lax
from jax.experimental import pallas as pl
from jax.experimental.pallas import tpu as pltpu
from jax.sharding import Mesh, PartitionSpec as P

PI_STEPS = 6
EXACT = lax.Precision.HIGHEST
F32 = jnp.float32
BF16 = jnp.bfloat16
SIZES = {"zl": 4, "y": 4, "c": 2, "zh": 2, "x": 4}
DP = ("zl", "y", "c")
TE = ("zh", "x")


def matmul(left, right):
    return jnp.dot(left, right, precision=EXACT, preferred_element_type=F32)


def shift(value, axis, k):
    n = SIZES[axis]
    return lax.ppermute(value, axis, [(i, (i - k) % n) for i in range(n)])


def all_sum(value, axis):
    if SIZES[axis] == 2:
        return value + shift(value, axis, 1)
    one, two, three = (shift(value, axis, k) for k in (1, 2, 3))
    return (value + two) + (one + three)


def scatter_sum(value, axis):
    n = SIZES[axis]
    moved = lax.all_to_all(value, axis, 0, 0, tiled=True)
    return moved.reshape(n, value.shape[0] // n, *value.shape[1:]).sum(0)


def gather(value, axis):
    n = SIZES[axis]
    rows = value.shape[0]
    me = lax.axis_index(axis)
    out = jnp.zeros((n * rows, *value.shape[1:]), value.dtype)
    out = lax.dynamic_update_slice_in_dim(out, value, me * rows, 0)
    for k in range(1, n):
        out = lax.dynamic_update_slice_in_dim(out, shift(value, axis, k), ((me + k) % n) * rows, 0)
    return out


def gather_dp(value):
    return gather(gather(gather(value, "zl"), "y"), "c")


def scatter_dp(value):
    return scatter_sum(scatter_sum(scatter_sum(value, "c"), "y"), "zl")


def sum_te(value):
    return all_sum(all_sum(value, "zh"), "x")


def power_kernel(kernel_ref, total_ref, col_ref, row_ref, ratio_ref):
    inv = 1.0 / total_ref[0, 0]
    rank = kernel_ref.shape[0]

    def to_row(col):
        return jnp.sum(kernel_ref[...] * col, axis=0, keepdims=True) * inv

    def to_col(row):
        return jnp.sum(kernel_ref[...] * row, axis=1, keepdims=True) * inv

    def unit(vec):
        return vec / jnp.sqrt(jnp.sum(vec * vec, keepdims=True) + 1e-12)

    col = jnp.full((rank, 1), 1.0, F32) / jnp.sqrt(F32(rank))
    for sweep in range(PI_STEPS // 2):
        row = unit(to_row(col))
        col = unit(to_col(row))
    last = to_row(col)
    eye = lax.broadcasted_iota(jnp.int32, (rank, rank), 0) == lax.broadcasted_iota(
        jnp.int32, (rank, rank), 1
    )
    row = jnp.sum(jnp.where(eye, col, 0.0), axis=0, keepdims=True)
    ratio = jnp.sum(row * last, keepdims=True)
    col_ref[...] = col
    row_ref[...] = row
    ratio_ref[...] = jnp.broadcast_to(ratio, ratio_ref.shape)


def leading(kernel, total):
    rank = kernel.shape[0]
    col, row, ratio = pl.pallas_call(
        power_kernel,
        out_shape=(
            jax.ShapeDtypeStruct((rank, 1), F32),
            jax.ShapeDtypeStruct((1, rank), F32),
            jax.ShapeDtypeStruct((8, 128), F32),
        ),
        in_specs=[
            pl.BlockSpec(memory_space=pltpu.VMEM),
            pl.BlockSpec(memory_space=pltpu.SMEM),
        ],
        out_specs=(
            pl.BlockSpec(memory_space=pltpu.VMEM),
            pl.BlockSpec(memory_space=pltpu.VMEM),
            pl.BlockSpec(memory_space=pltpu.VMEM),
        ),
        compiler_params=pltpu.CompilerParams(vmem_limit_bytes=24 * 1024 * 1024),
    )(kernel, total.reshape(1, 1))
    return row[0], ratio[0, 0]


def body(layer_inputs, out_grads, basis, first, second):
    rank = basis.shape[1]
    own = rank // 32
    zl, y, c = (lax.axis_index(a) for a in DP)
    inner = (c * 4 + y) * 4 + zl
    row_start = ((zl * 4 + y) * 2 + c) * own

    def to_inner(value):
        lead = value.shape[:-1]
        split = value.reshape(*lead, 4, 4, 2, own)
        k = len(lead)
        return split.transpose(*range(k), k + 2, k + 1, k, k + 3).reshape(*lead, rank)

    def to_outer(value):
        lead = value.shape[:-1]
        split = value.reshape(*lead, 2, 4, 4, own)
        k = len(lead)
        return split.transpose(*range(k), k + 2, k + 1, k, k + 3).reshape(*lead, rank)

    basis_low = basis.astype(BF16)
    score_part = jnp.dot(layer_inputs, basis_low, preferred_element_type=F32)
    score_own = all_sum(scatter_sum(score_part, "x"), "zh")
    scores = gather(to_inner(score_own.astype(BF16)), "x")

    grad_part = lax.dot_general(
        scores, out_grads, (((0,), (0,)), ((), ())), preferred_element_type=F32
    )
    grad_own = scatter_dp(grad_part)
    grad_low = gather_dp(grad_own.astype(BF16))
    back_part = lax.dot_general(
        out_grads, grad_low, (((1,), (1,)), ((), ())), preferred_element_type=F32
    )
    back_own = all_sum(scatter_sum(back_part, "x"), "zh")
    backward = gather(back_own.astype(BF16), "x")
    tangent_part = lax.dot_general(
        layer_inputs, backward, (((0,), (0,)), ((), ())), preferred_element_type=F32
    )
    tangent = gather_dp(scatter_dp(tangent_part))

    basis_own = lax.dynamic_slice_in_dim(basis, row_start, own, 1)
    gram_own = sum_te(lax.dot_general(basis_own, basis, (((0,), (0,)), ((), ())), precision=EXACT))
    tan_own = lax.dynamic_slice_in_dim(tangent, inner * own, own, 1)
    slab = jnp.concatenate([tangent, basis], axis=1)
    pair = sum_te(lax.dot_general(tan_own, slab, (((0,), (0,)), ((), ())), precision=EXACT))
    pairs = gather_dp(pair)
    gram = gather_dp(gram_own)
    gram = gram.reshape(2, 4, 4, own, rank).transpose(2, 1, 0, 3, 4).reshape(rank, rank)
    tan_gram = pairs[:, :rank]
    coup_t = pairs[:, rank:]
    kernel = tan_gram - lax.dot_general(
        2.0 * coup_t - matmul(coup_t, gram), coup_t, (((1,), (1,)), ((), ())), precision=EXACT
    )
    total = jnp.trace(kernel)
    vec_in, ratio = leading(kernel, total)
    vector = to_outer(vec_in)
    theta = 4.0 * jnp.sqrt(ratio)
    sigma = jnp.sqrt(total * ratio + 1e-06)
    cosine_val = jnp.cos(theta)
    sine_val = jnp.sin(theta)

    coup_vec = matmul(vec_in, coup_t)
    left_part = (matmul(tangent, vec_in) - matmul(basis, coup_vec)) / sigma
    basis_dir = matmul(basis, vector)
    new_basis = basis + jnp.outer((cosine_val - 1.0) * basis_dir + sine_val * left_part, vector)
    tail = (cosine_val - 1.0) * matmul(gram, vector) + (sine_val / sigma) * (
        coup_vec - matmul(gram, coup_vec)
    )
    vector_own = lax.dynamic_slice_in_dim(vector, row_start, own, 0)
    gram_rows = lax.dynamic_slice_in_dim(gram, row_start, own, 0)
    rot_own = gram_rows + jnp.outer(vector_own, tail)

    left_low = left_part.astype(BF16)
    probe_part = jnp.dot(layer_inputs, left_low, preferred_element_type=F32)
    probe = sum_te(probe_part).astype(BF16)
    along_part = jnp.dot(probe, out_grads, preferred_element_type=F32)
    lead_part = matmul(vector_own, grad_own)
    push_part = (cosine_val - 1.0) * lead_part + sine_val * along_part
    push = all_sum(all_sum(all_sum(push_part, "c"), "y"), "zl")

    def rows_outer(value):
        return value.reshape(2, 4, 4, own, value.shape[-1]).transpose(2, 1, 0, 3, 4).reshape(
            rank, value.shape[-1]
        )

    rot_in = to_inner(rot_own)
    rotated_m = matmul(rot_in, gather_dp(first))
    rotated_v = matmul(rot_in * rot_in, gather_dp(second))
    grad_new = grad_own + jnp.outer(vector_own, push)
    new_first = 0.9 * rotated_m + 0.1 * grad_new
    new_second = 0.95 * rotated_v + 0.05 * grad_new * grad_new
    update = new_first / (jnp.sqrt(new_second) + 1e-06)
    return (new_basis, new_first, new_second, update)


def solution(mesh):
    fine = Mesh(mesh.devices.reshape(4, 4, 2, 2, 4), DP + TE)
    return jax.shard_map(
        body,
        mesh=fine,
        in_specs=(P(DP, TE), P(DP, TE), P(TE, None), P(DP, TE), P(DP, TE)),
        out_specs=(P(TE, None), P(DP, TE), P(DP, TE), P(DP, TE)),
        check_vma=False,
    )
```

```python
import jax
import jax.numpy as jnp
from jax import lax
from jax.experimental import pallas as pl
from jax.experimental.pallas import tpu as pltpu
from jax.sharding import Mesh, PartitionSpec as P

PI_STEPS = 6
EXACT = lax.Precision.HIGHEST
F32 = jnp.float32
BF16 = jnp.bfloat16
SIZES = {"zl": 4, "y": 4, "c": 2, "zh": 2, "x": 4}
DP = ("zl", "y", "c")
TE = ("zh", "x")


def matmul(left, right):
    return jnp.dot(left, right, precision=EXACT, preferred_element_type=F32)


def shift(value, axis, k):
    n = SIZES[axis]
    return lax.ppermute(value, axis, [(i, (i - k) % n) for i in range(n)])


def all_sum(value, axis):
    if SIZES[axis] == 2:
        return value + shift(value, axis, 1)
    one, two, three = (shift(value, axis, k) for k in (1, 2, 3))
    return (value + two) + (one + three)


def scatter_sum(value, axis):
    n = SIZES[axis]
    moved = lax.all_to_all(value, axis, 0, 0, tiled=True)
    return moved.reshape(n, value.shape[0] // n, *value.shape[1:]).sum(0)


def stack(value, axis):
    n = SIZES[axis]
    me = lax.axis_index(axis)
    out = jnp.zeros((n, *value.shape), value.dtype)
    out = lax.dynamic_update_slice_in_dim(out, value[None], me, 0)
    for k in range(1, n):
        out = lax.dynamic_update_slice_in_dim(out, shift(value, axis, k)[None], (me + k) % n, 0)
    return out


def stack_dp(value):
    return stack(stack(stack(value, "zl"), "y"), "c")


def sum_te(value):
    return all_sum(all_sum(value, "zh"), "x")


def power_kernel(kernel_ref, total_ref, col_ref, row_ref, ratio_ref):
    inv = 1.0 / total_ref[0, 0]
    rank = kernel_ref.shape[0]

    def to_row(col):
        return jnp.sum(kernel_ref[...] * col, axis=0, keepdims=True) * inv

    def to_col(row):
        return jnp.sum(kernel_ref[...] * row, axis=1, keepdims=True) * inv

    def unit(vec):
        return vec / jnp.sqrt(jnp.sum(vec * vec, keepdims=True) + 1e-12)

    col = jnp.full((rank, 1), 1.0, F32) / jnp.sqrt(F32(rank))
    for sweep in range(PI_STEPS // 2):
        row = unit(to_row(col))
        col = unit(to_col(row))
    last = to_row(col)
    eye = lax.broadcasted_iota(jnp.int32, (rank, rank), 0) == lax.broadcasted_iota(
        jnp.int32, (rank, rank), 1
    )
    row = jnp.sum(jnp.where(eye, col, 0.0), axis=0, keepdims=True)
    ratio = jnp.sum(row * last, keepdims=True)
    col_ref[...] = col
    row_ref[...] = row
    ratio_ref[...] = jnp.broadcast_to(ratio, ratio_ref.shape)


def leading(kernel, total):
    rank = kernel.shape[0]
    col, row, ratio = pl.pallas_call(
        power_kernel,
        out_shape=(
            jax.ShapeDtypeStruct((rank, 1), F32),
            jax.ShapeDtypeStruct((1, rank), F32),
            jax.ShapeDtypeStruct((8, 128), F32),
        ),
        in_specs=[
            pl.BlockSpec(memory_space=pltpu.VMEM),
            pl.BlockSpec(memory_space=pltpu.SMEM),
        ],
        out_specs=(
            pl.BlockSpec(memory_space=pltpu.VMEM),
            pl.BlockSpec(memory_space=pltpu.VMEM),
            pl.BlockSpec(memory_space=pltpu.VMEM),
        ),
        compiler_params=pltpu.CompilerParams(vmem_limit_bytes=24 * 1024 * 1024),
    )(kernel, total.reshape(1, 1))
    return row[0], ratio[0, 0]


def back_kernel(grads_ref, low_ref, out_ref):
    rows = low_ref.shape[3]
    for y in range(4):
        total = jnp.zeros((out_ref.shape[0], rows), F32)
        for c in range(2):
            for zl in range(4):
                total += lax.dot_general(
                    grads_ref[c, zl],
                    low_ref[c, y, zl],
                    (((1,), (1,)), ((), ())),
                    preferred_element_type=F32,
                )
        out_ref[:, y * rows : (y + 1) * rows] = total


def back_product(grads, low):
    tokens = grads.shape[2]
    return pl.pallas_call(
        back_kernel,
        out_shape=jax.ShapeDtypeStruct((tokens, 4 * low.shape[3]), F32),
        in_specs=[pl.BlockSpec(memory_space=pltpu.VMEM)] * 2,
        out_specs=pl.BlockSpec(memory_space=pltpu.VMEM),
        compiler_params=pltpu.CompilerParams(vmem_limit_bytes=24 * 1024 * 1024),
    )(grads, low)


CZ = ("c", "zl")


def body(layer_inputs, out_grads, basis, first, second):
    tokens, feats = layer_inputs.shape
    cols = out_grads.shape[1] // 8
    rank = basis.shape[1]
    own = rank // 32
    zl, y, c = (lax.axis_index(a) for a in DP)
    piece = (c * 4 + y) * 4 + zl
    part = feats // 32

    def to_inner(value):
        lead = value.shape[:-1]
        k = len(lead)
        split = value.reshape(*lead, 4, 4, 2, own)
        return split.transpose(*range(k), k + 1, k + 2, k, k + 3).reshape(*lead, rank)

    def to_outer(value):
        lead = value.shape[:-1]
        k = len(lead)
        split = value.reshape(*lead, 4, 2, 4, own)
        return split.transpose(*range(k), k + 2, k, k + 1, k + 3).reshape(*lead, rank)

    grads = out_grads.reshape(tokens, 8, cols).transpose(1, 0, 2)
    grads_all = lax.all_to_all(grads, CZ, 0, 0, tiled=True).reshape(8 * tokens, cols)
    inputs = layer_inputs.reshape(tokens, 2, 4, 4, part).transpose(1, 3, 0, 2, 4)
    inputs_all = lax.all_to_all(
        inputs.reshape(8, tokens, 4 * part), CZ, 0, 0, tiled=True
    ).reshape(8 * tokens, 4 * part)
    moments = jnp.stack([first, second]).reshape(2, own, 8, cols).transpose(2, 0, 1, 3)
    moments = lax.all_to_all(moments, CZ, 0, 0, tiled=True)
    moments = stack(moments, "y")
    first_all = moments[:, :, 0].reshape(rank, cols)
    second_all = moments[:, :, 1].reshape(rank, cols)

    basis_low = basis.astype(BF16)
    score_part = jnp.dot(layer_inputs, basis_low, preferred_element_type=F32)
    score_own = all_sum(scatter_sum(score_part, "x"), "zh")
    scores = stack(to_inner(score_own.astype(BF16)), "x").reshape(tokens, rank)
    scores_all = stack(stack(scores, "zl"), "c").reshape(8 * tokens, rank)

    grad_part = lax.dot_general(
        scores_all, grads_all, (((0,), (0,)), ((), ())), preferred_element_type=F32
    )
    grad_own = scatter_sum(grad_part, "y")
    grad_low = stack_dp(grad_own.astype(BF16))
    back_part = back_product(grads.reshape(2, 4, tokens, cols), grad_low)
    back_own = all_sum(scatter_sum(back_part, "x"), "zh")
    backward = stack(back_own.astype(BF16), "x").reshape(tokens, rank)
    backward_all = stack(stack(backward, "zl"), "c").reshape(8 * tokens, rank)
    tangent_part = lax.dot_general(
        inputs_all, backward_all, (((0,), (0,)), ((), ())), preferred_element_type=F32
    )
    tangent = stack_dp(scatter_sum(tangent_part, "y")).reshape(feats, rank)

    basis_in = to_inner(basis)
    basis_own = lax.dynamic_slice_in_dim(basis_in, piece * own, own, 1)
    gram_own = sum_te(
        lax.dot_general(basis_own, basis_in, (((0,), (0,)), ((), ())), precision=EXACT)
    )
    gram = stack_dp(gram_own).reshape(rank, rank)
    tan_own = lax.dynamic_slice_in_dim(tangent, piece * own, own, 1)
    pair = sum_te(
        jnp.concatenate(
            [
                lax.dot_general(tan_own, tangent, (((0,), (0,)), ((), ())), precision=EXACT),
                lax.dot_general(tan_own, basis_in, (((0,), (0,)), ((), ())), precision=EXACT),
            ],
            axis=1,
        )
    )
    pairs = stack_dp(pair).reshape(rank, 2 * rank)
    tan_gram = pairs[:, :rank]
    coup_t = pairs[:, rank:]
    kernel = tan_gram - lax.dot_general(
        2.0 * coup_t - matmul(coup_t, gram), coup_t, (((1,), (1,)), ((), ())), precision=EXACT
    )
    total = jnp.trace(kernel)
    vec_in, ratio = leading(kernel, total)
    vector = to_outer(vec_in)
    theta = 4.0 * jnp.sqrt(ratio)
    sigma = jnp.sqrt(total * ratio + 1e-06)
    cosine_val = jnp.cos(theta)
    sine_val = jnp.sin(theta)

    coup_vec = matmul(vec_in, coup_t)
    left_part = (matmul(tangent, vec_in) - matmul(basis_in, coup_vec)) / sigma
    basis_dir = matmul(basis_in, vec_in)
    new_basis = basis + jnp.outer((cosine_val - 1.0) * basis_dir + sine_val * left_part, vector)
    tail = (cosine_val - 1.0) * matmul(gram, vec_in) + (sine_val / sigma) * (
        coup_vec - matmul(gram, coup_vec)
    )
    block = 8 * own
    vec_own = lax.dynamic_slice_in_dim(vec_in, y * block, block, 0)
    rot_own = lax.dynamic_slice_in_dim(gram, y * block, block, 0) + jnp.outer(vec_own, tail)

    left_low = left_part.astype(BF16)
    probe_part = jnp.dot(layer_inputs, left_low, preferred_element_type=F32)
    probe = sum_te(probe_part).astype(BF16)
    probe_all = lax.all_to_all(
        jnp.broadcast_to(probe[None], (8, tokens)), CZ, 0, 0, tiled=True
    ).reshape(8 * tokens)
    along_part = jnp.dot(probe_all, grads_all, preferred_element_type=F32)
    lead_part = matmul(vec_own, grad_own)
    push = all_sum((cosine_val - 1.0) * lead_part + sine_val * along_part, "y")

    rotated_m = matmul(rot_own, first_all)
    rotated_v = matmul(rot_own * rot_own, second_all)
    grad_new = grad_own + jnp.outer(vec_own, push)
    moved = jnp.stack(
        [0.9 * rotated_m + 0.1 * grad_new, 0.95 * rotated_v + 0.05 * grad_new * grad_new]
    )
    moved = moved.reshape(2, 8, own, cols).transpose(1, 0, 2, 3)
    moved = lax.all_to_all(moved, CZ, 0, 0, tiled=True)
    moved = moved.transpose(1, 2, 0, 3).reshape(2, own, 8 * cols)
    new_first, new_second = moved[0], moved[1]
    update = new_first / (jnp.sqrt(new_second) + 1e-06)
    return (new_basis, new_first, new_second, update)


def solution(mesh):
    fine = Mesh(mesh.devices.reshape(4, 4, 2, 2, 4), DP + TE)
    return jax.shard_map(
        body,
        mesh=fine,
        in_specs=(P(DP, TE), P(DP, TE), P(TE, None), P(DP, TE), P(DP, TE)),
        out_specs=(P(TE, None), P(DP, TE), P(DP, TE), P(DP, TE)),
        check_vma=False,
    )
```

```python
import jax
import jax.numpy as jnp
from jax import lax
from jax.experimental import pallas as pl
from jax.experimental.pallas import tpu as pltpu
from jax.sharding import Mesh, PartitionSpec as P

PI_STEPS = 6
EXACT = lax.Precision.HIGHEST
F32 = jnp.float32
BF16 = jnp.bfloat16
SIZES = {"zl": 4, "y": 4, "c": 2, "zh": 2, "x": 4}
DP = ("zl", "y", "c")
TE = ("zh", "x")


def matmul(left, right):
    return jnp.dot(left, right, precision=EXACT, preferred_element_type=F32)


def shift(value, axis, k):
    n = SIZES[axis]
    return lax.ppermute(value, axis, [(i, (i - k) % n) for i in range(n)])


def all_sum(value, axis):
    if SIZES[axis] == 2:
        return value + shift(value, axis, 1)
    one, two, three = (shift(value, axis, k) for k in (1, 2, 3))
    return (value + two) + (one + three)


def scatter_sum(value, axis):
    n = SIZES[axis]
    moved = lax.all_to_all(value, axis, 0, 0, tiled=True)
    return moved.reshape(n, value.shape[0] // n, *value.shape[1:]).sum(0)


def stack(value, axis):
    n = SIZES[axis]
    me = lax.axis_index(axis)
    out = jnp.zeros((n, *value.shape), value.dtype)
    out = lax.dynamic_update_slice_in_dim(out, value[None], me, 0)
    for k in range(1, n):
        out = lax.dynamic_update_slice_in_dim(out, shift(value, axis, k)[None], (me + k) % n, 0)
    return out


def stack_dp(value):
    return stack(stack(stack(value, "zl"), "y"), "c")


def sum_te(value):
    return all_sum(all_sum(value, "zh"), "x")


def finish_kernel(
    pairs_ref, gram_ref, tangent_ref, basis_ref, inputs_ref, vec_ref, tail_ref, step_ref, probe_ref, scal_ref
):
    rank = gram_ref.shape[0]
    blocks = rank // 128

    def exact(left, right, dims):
        return lax.dot_general(left, right, (dims, ((), ())), precision=EXACT, preferred_element_type=F32)

    nn, nt = ((1,), (0,)), ((1,), (1,))
    coup_t = pairs_ref[:, :, rank:].reshape(rank, rank)
    gram = gram_ref[...]
    mixed = 2.0 * coup_t - exact(coup_t, gram, nn)
    kernel = pairs_ref[:, :, :rank].reshape(rank, rank) - exact(mixed, coup_t, nt)
    rows = lax.broadcasted_iota(jnp.int32, (rank, rank), 0)
    lanes = lax.broadcasted_iota(jnp.int32, (rank, rank), 1)
    eye = rows == lanes
    total = jnp.sum(jnp.where(eye, kernel, 0.0), keepdims=True)
    normed = kernel / total

    def to_row(col):
        return jnp.sum(normed * col, axis=0, keepdims=True)

    def to_col(row):
        return jnp.sum(normed * row, axis=1, keepdims=True)

    def unit(vec):
        return vec / jnp.sqrt(jnp.sum(vec * vec, keepdims=True) + 1e-12)

    col = jnp.full((rank, 1), 1.0, F32) / jnp.sqrt(F32(rank))
    for sweep in range(PI_STEPS // 2):
        col = unit(to_col(unit(to_row(col))))
    last = to_row(col)
    row = jnp.sum(jnp.where(eye, col, 0.0), axis=0, keepdims=True)
    ratio = jnp.sum(row * last, keepdims=True)
    own = rank // 32
    group = lanes // own
    source = ((group // 2) % 4) * 8 + (group % 2) * 4 + group // 8
    vector = jnp.sum(jnp.where(rows == source * own + lanes % own, col, 0.0), axis=0, keepdims=True)
    theta = 4.0 * jnp.sqrt(ratio)
    sigma = jnp.sqrt(total * ratio + 1e-06)
    shrink = jnp.cos(theta) - 1.0
    sine = jnp.sin(theta)

    def tall(vec):
        return jnp.broadcast_to(vec, (8, vec.shape[1]))

    coup_vec = exact(tall(row), coup_t, nn)
    both = exact(jnp.concatenate([tall(vector), coup_vec], axis=0), gram, nn)
    tail = shrink * both[:8] + (sine / sigma) * (coup_vec - both[8:])
    turned = exact(jnp.concatenate([coup_vec, tall(vector)], axis=0), basis_ref[...], nt)
    left = (exact(tall(row), tangent_ref[...], nt) - turned[:8]) / sigma
    probe_ref[...] = lax.dot_general(
        left.astype(BF16), inputs_ref[...], (nt, ((), ())), preferred_element_type=F32
    )
    vec_ref[...] = tall(vector)
    tail_ref[...] = tail
    step_ref[...] = shrink * turned[8:] + sine * left
    lane = lax.broadcasted_iota(jnp.int32, scal_ref.shape, 1)
    scal_ref[...] = jnp.where(lane == 0, shrink, sine)


def finish(pairs, gram, tangent, basis, inputs):
    rank = gram.shape[0]
    vmem = pl.BlockSpec(memory_space=pltpu.VMEM)
    return pl.pallas_call(
        finish_kernel,
        out_shape=(
            jax.ShapeDtypeStruct((8, rank), F32),
            jax.ShapeDtypeStruct((8, rank), F32),
            jax.ShapeDtypeStruct((8, tangent.shape[0]), F32),
            jax.ShapeDtypeStruct((8, inputs.shape[0]), F32),
            jax.ShapeDtypeStruct((8, 128), F32),
        ),
        in_specs=[vmem] * 5,
        out_specs=(vmem,) * 5,
        compiler_params=pltpu.CompilerParams(vmem_limit_bytes=40 * 1024 * 1024),
    )(pairs, gram, tangent, basis, inputs)


def back_kernel(grads_ref, low_ref, out_ref):
    rows = low_ref.shape[3]
    for y in range(4):
        total = jnp.zeros((out_ref.shape[0], rows), F32)
        for c in range(2):
            for zl in range(4):
                total += lax.dot_general(
                    grads_ref[c, zl],
                    low_ref[c, y, zl],
                    (((1,), (1,)), ((), ())),
                    preferred_element_type=F32,
                )
        out_ref[:, y * rows : (y + 1) * rows] = total


def back_product(grads, low):
    tokens = grads.shape[2]
    return pl.pallas_call(
        back_kernel,
        out_shape=jax.ShapeDtypeStruct((tokens, 4 * low.shape[3]), F32),
        in_specs=[pl.BlockSpec(memory_space=pltpu.VMEM)] * 2,
        out_specs=pl.BlockSpec(memory_space=pltpu.VMEM),
        compiler_params=pltpu.CompilerParams(vmem_limit_bytes=24 * 1024 * 1024),
    )(grads, low)


CZ = ("c", "zl")


def body(layer_inputs, out_grads, basis, first, second):
    tokens, feats = layer_inputs.shape
    cols = out_grads.shape[1] // 8
    rank = basis.shape[1]
    own = rank // 32
    zl, y, c = (lax.axis_index(a) for a in DP)
    row_start = ((zl * 4 + y) * 2 + c) * own
    part = feats // 32

    def to_inner(value):
        lead = value.shape[:-1]
        k = len(lead)
        split = value.reshape(*lead, 4, 4, 2, own)
        return split.transpose(*range(k), k + 1, k + 2, k, k + 3).reshape(*lead, rank)

    grads = out_grads.reshape(tokens, 8, cols).transpose(1, 0, 2)
    grads_all = lax.all_to_all(grads, CZ, 0, 0, tiled=True).reshape(8 * tokens, cols)
    inputs = layer_inputs.reshape(tokens, 2, 4, 4, part).transpose(1, 3, 0, 2, 4)
    inputs_all = lax.all_to_all(
        inputs.reshape(8, tokens, 4 * part), CZ, 0, 0, tiled=True
    ).reshape(8 * tokens, 4 * part)
    first_all = lax.all_gather(first, DP, axis=0, tiled=True)
    second_all = lax.all_gather(second, DP, axis=0, tiled=True)
    gram = lax.psum(matmul(basis.T, basis), TE)

    basis_low = basis.astype(BF16)
    score_part = jnp.dot(layer_inputs, basis_low, preferred_element_type=F32)
    score_own = all_sum(scatter_sum(score_part, "x"), "zh")
    scores = stack(to_inner(score_own.astype(BF16)), "x").reshape(tokens, rank)
    scores_all = stack(stack(scores, "zl"), "c").reshape(8 * tokens, rank)

    grad_part = lax.dot_general(
        scores_all, grads_all, (((0,), (0,)), ((), ())), preferred_element_type=F32
    )
    grad_own = scatter_sum(grad_part, "y")
    grad_low = stack_dp(grad_own.astype(BF16))
    grad_rows = lax.all_to_all(grad_own.reshape(8, own, cols), CZ, 0, 0, tiled=True)
    grad_rows = grad_rows.transpose(1, 0, 2).reshape(own, 8 * cols)
    back_part = back_product(grads.reshape(2, 4, tokens, cols), grad_low)
    back_own = all_sum(scatter_sum(back_part, "x"), "zh")
    backward = stack(back_own.astype(BF16), "x").reshape(tokens, rank)
    backward_all = stack(stack(backward, "zl"), "c").reshape(8 * tokens, rank)
    tangent_part = lax.dot_general(
        inputs_all, backward_all, (((0,), (0,)), ((), ())), preferred_element_type=F32
    )
    tangent = stack_dp(scatter_sum(tangent_part, "y")).reshape(feats, rank)

    piece = (c * 4 + y) * 4 + zl
    tan_own = lax.dynamic_slice_in_dim(tangent, piece * own, own, 1)
    pair = sum_te(
        jnp.concatenate(
            [
                lax.dot_general(tan_own, tangent, (((0,), (0,)), ((), ())), precision=EXACT),
                lax.dot_general(tan_own, basis, (((0,), (0,)), ((), ())), precision=EXACT),
            ],
            axis=1,
        )
    )
    pairs = stack_dp(pair).reshape(32, own, 2 * rank)
    vec, tail, step, probe_part, scal = finish(pairs, gram, tangent, basis, layer_inputs)
    vector = vec[0]
    new_basis = basis + jnp.outer(step[0], vector)
    probe = sum_te(probe_part)[0].astype(BF16)
    vec_own = lax.dynamic_slice_in_dim(vector, row_start, own, 0)
    rot_own = lax.dynamic_slice_in_dim(gram, row_start, own, 0) + jnp.outer(vec_own, tail[0])
    along_part = jnp.dot(probe, out_grads, preferred_element_type=F32)
    lead_part = jnp.sum(vec_own[:, None] * grad_rows, axis=0)
    push_part = scal[0, 0] * lead_part + scal[0, 1] * along_part
    push = lax.all_to_all(
        jnp.broadcast_to(push_part.reshape(1, -1, 128), (32, push_part.size // 128, 128)),
        DP, 0, 0, tiled=True,
    ).sum(0).reshape(push_part.size)

    rotated_m = matmul(rot_own, first_all)
    rotated_v = matmul(rot_own * rot_own, second_all)
    grad_new = grad_rows + jnp.outer(vec_own, push)
    new_first = 0.9 * rotated_m + 0.1 * grad_new
    new_second = 0.95 * rotated_v + 0.05 * grad_new * grad_new
    update = new_first / (jnp.sqrt(new_second) + 1e-06)
    return (new_basis, new_first, new_second, update)


def solution(mesh):
    fine = Mesh(mesh.devices.reshape(4, 4, 2, 2, 4), DP + TE)
    return jax.shard_map(
        body,
        mesh=fine,
        in_specs=(P(DP, TE), P(DP, TE), P(TE, None), P(DP, TE), P(DP, TE)),
        out_specs=(P(TE, None), P(DP, TE), P(DP, TE), P(DP, TE)),
        check_vma=False,
    )
```

```python
import jax
import jax.numpy as jnp
from jax import lax
from jax.experimental import pallas as pl
from jax.experimental.pallas import tpu as pltpu
from jax.sharding import Mesh, PartitionSpec as P

PI_STEPS = 6
EXACT = lax.Precision.HIGHEST
F32 = jnp.float32
BF16 = jnp.bfloat16
SIZES = {"zl": 4, "y": 4, "c": 2, "zh": 2, "x": 4}
DP = ("zl", "y", "c")
TE = ("zh", "x")


def shift(value, axis, k):
    n = SIZES[axis]
    return lax.ppermute(value, axis, [(i, (i - k) % n) for i in range(n)])


def all_sum(value, axis):
    if SIZES[axis] == 2:
        return value + shift(value, axis, 1)
    one, two, three = (shift(value, axis, k) for k in (1, 2, 3))
    return (value + two) + (one + three)


def scatter_sum(value, axis):
    n = SIZES[axis]
    moved = lax.all_to_all(value, axis, 0, 0, tiled=True)
    return moved.reshape(n, value.shape[0] // n, *value.shape[1:]).sum(0)


def scatter_near(value, axis):
    n = SIZES[axis]
    me = lax.axis_index(axis)
    rows = value.shape[0] // n

    def mine(k):
        return lax.dynamic_slice_in_dim(value, ((me + k) % n) * rows, rows, 0)

    one, two, three = (
        lax.ppermute(mine(k), axis, [(i, (i + k) % n) for i in range(n)]) for k in (1, 2, 3)
    )
    return (mine(0) + two) + (one + three)


def stack(value, axis, at_once=False):
    n = SIZES[axis]
    if at_once:
        many = jnp.broadcast_to(value[None], (n, *value.shape))
        return lax.all_to_all(many, axis, 0, 0, tiled=True)
    me = lax.axis_index(axis)
    if n == 2:
        other = shift(value, axis, 1)
        return jnp.where(me == 0, jnp.stack([value, other]), jnp.stack([other, value]))
    out = jnp.zeros((n, *value.shape), value.dtype)
    out = lax.dynamic_update_slice_in_dim(out, value[None], me, 0)
    for k in range(1, n):
        out = lax.dynamic_update_slice_in_dim(out, shift(value, axis, k)[None], (me + k) % n, 0)
    return out


def stack_dp(value, at_once=False):
    value = stack(value, "zl")
    value = stack(value, "y", at_once)
    return stack(value, "c")


def sum_te(value):
    return all_sum(all_sum(value, "zh"), "x")


NN, NT, TN = ((1,), (0,)), ((1,), (1,)), ((0,), (0,))


def exact(left, right, dims):
    return lax.dot_general(left, right, (dims, ((), ())), precision=EXACT, preferred_element_type=F32)


def low(left, right, dims):
    return lax.dot_general(left, right, (dims, ((), ())), preferred_element_type=F32)


def finish_kernel(
    place_ref, pairs_ref, tangent_ref, basis_ref, inputs_ref,
    vec_ref, own_ref, rot_ref, step_ref, probe_ref, scal_ref,
    kernel_ref, col_ref,
):
    rank = kernel_ref.shape[0]
    own = rank // 32
    coup = pl.ds(rank, rank)
    wide = pl.ds(2 * rank, rank)

    def fill(i, carry):
        some = pl.ds(i * 8, 8)
        mine = pairs_ref[some, :, coup].reshape(8 * own, rank)
        mixed = 2.0 * mine - exact(mine, pairs_ref[:, :, wide].reshape(rank, rank), NN)
        rows = pairs_ref[some, :, pl.ds(0, rank)].reshape(8 * own, rank)
        kernel_ref[pl.ds(i * 8 * own, 8 * own), :] = rows - exact(
            mixed, pairs_ref[:, :, coup].reshape(rank, rank), NT
        )
        return carry

    lax.fori_loop(0, 4, fill, 0)
    rows = lax.broadcasted_iota(jnp.int32, (rank, rank), 0)
    lanes = lax.broadcasted_iota(jnp.int32, (rank, rank), 1)
    total = jnp.sum(jnp.where(rows == lanes, kernel_ref[...], 0.0), keepdims=True)
    inv = 1.0 / total

    def to_row(col):
        return jnp.sum(kernel_ref[...] * col, axis=0, keepdims=True) * inv

    def to_col(row):
        return jnp.sum(kernel_ref[...] * row, axis=1, keepdims=True) * inv

    def unit(vec):
        return vec / jnp.sqrt(jnp.sum(vec * vec, keepdims=True) + 1e-12)

    col_ref[...] = jnp.full((rank, 1), 1.0, F32) / jnp.sqrt(F32(rank))

    def sweep(i, carry):
        col_ref[...] = unit(to_col(unit(to_row(col_ref[...]))))
        return carry

    lax.fori_loop(0, PI_STEPS // 2, sweep, 0)
    col = col_ref[...]
    last = to_row(col)
    row = jnp.sum(jnp.where(rows == lanes, col, 0.0), axis=0, keepdims=True)
    ratio = jnp.sum(row * last, keepdims=True)
    group = lanes // own
    source = ((group // 2) % 4) * 8 + (group % 2) * 4 + group // 8
    vector = jnp.sum(jnp.where(rows == source * own + lanes % own, col, 0.0), axis=0, keepdims=True)
    theta = 4.0 * jnp.sqrt(ratio)
    sigma = jnp.sqrt(total * ratio + 1e-06)
    shrink = jnp.cos(theta) - 1.0
    sine = jnp.sin(theta)

    def tall(vec):
        return jnp.broadcast_to(vec, (8, vec.shape[1]))

    coup_vec = exact(tall(row), pairs_ref[:, :, coup].reshape(rank, rank), NN)
    both = exact(
        jnp.concatenate([tall(vector), coup_vec], axis=0), pairs_ref[:, :, wide].reshape(rank, rank), NN
    )
    tail = (shrink * both[:8] + (sine / sigma) * (coup_vec - both[8:]))[:1]
    turned = exact(jnp.concatenate([coup_vec, tall(vector)], axis=0), basis_ref[...], NT)
    left = (exact(tall(row), tangent_ref[...], NT) - turned[:8]) / sigma
    probe_ref[...] = low(left.astype(BF16), inputs_ref[...], NT)
    vec_ref[...] = tall(vector)
    step_ref[...] = shrink * turned[8:] + sine * left
    lane = lax.broadcasted_iota(jnp.int32, scal_ref.shape, 1)
    scal_ref[...] = jnp.where(lane == 0, shrink, sine)
    y = place_ref[0]
    own_ref[...] = col_ref[pl.ds(pl.multiple_of(y * 8 * own, 8 * own), 8 * own), :]
    for c in range(2):
        for zl in range(4):
            some = pl.ds((c * 4 + zl) * own, own)
            rot_ref[some, :] = pairs_ref[zl * 8 + y * 2 + c, :, wide] + own_ref[some, :] * tail


def finish(place, pairs, tangent, basis, inputs):
    rank = basis.shape[1]
    vmem = pl.BlockSpec(memory_space=pltpu.VMEM)
    return pl.pallas_call(
        finish_kernel,
        out_shape=(
            jax.ShapeDtypeStruct((8, rank), F32),
            jax.ShapeDtypeStruct((rank // 4, 1), F32),
            jax.ShapeDtypeStruct((rank // 4, rank), F32),
            jax.ShapeDtypeStruct((8, tangent.shape[0]), F32),
            jax.ShapeDtypeStruct((8, inputs.shape[0]), F32),
            jax.ShapeDtypeStruct((8, 128), F32),
        ),
        in_specs=[pl.BlockSpec(memory_space=pltpu.SMEM)] + [vmem] * 4,
        out_specs=(vmem,) * 6,
        scratch_shapes=[pltpu.VMEM((rank, rank), F32), pltpu.VMEM((rank, 1), F32)],
        compiler_params=pltpu.CompilerParams(vmem_limit_bytes=40 * 1024 * 1024),
    )(place, pairs, tangent, basis, inputs)


def turn_kernel(rot_ref, moments_ref, out_ref):
    for which in range(2):
        rows = jnp.concatenate(
            [
                moments_ref[y, c, zl, which]
                for zl in range(4)
                for y in range(4)
                for c in range(2)
            ],
            axis=0,
        )
        rot = rot_ref[...]
        out_ref[which] = exact(rot if which == 0 else rot * rot, rows, NN)


def turn(rot, moments):
    cols = moments.shape[-1]
    vmem = pl.BlockSpec(memory_space=pltpu.VMEM)
    return pl.pallas_call(
        turn_kernel,
        out_shape=jax.ShapeDtypeStruct((2, rot.shape[0], cols), F32),
        in_specs=[vmem] * 2,
        out_specs=vmem,
        compiler_params=pltpu.CompilerParams(vmem_limit_bytes=24 * 1024 * 1024),
    )(rot, moments)


def back_kernel(grads_ref, low_ref, out_ref):
    rows = low_ref.shape[3]
    for y in range(4):
        total = jnp.zeros((out_ref.shape[0], rows), F32)
        for c in range(2):
            for zl in range(4):
                total += low(grads_ref[c, zl], low_ref[c, y, zl], NT)
        out_ref[:, y * rows : (y + 1) * rows] = total


def back_product(grads, low_rows):
    tokens = grads.shape[2]
    vmem = pl.BlockSpec(memory_space=pltpu.VMEM)
    return pl.pallas_call(
        back_kernel,
        out_shape=jax.ShapeDtypeStruct((tokens, 4 * low_rows.shape[3]), F32),
        in_specs=[vmem] * 2,
        out_specs=vmem,
        compiler_params=pltpu.CompilerParams(vmem_limit_bytes=24 * 1024 * 1024),
    )(grads, low_rows)


CZ = ("c", "zl")


def body(layer_inputs, out_grads, basis, first, second):
    tokens, feats = layer_inputs.shape
    cols = out_grads.shape[1] // 8
    rank = basis.shape[1]
    own = rank // 32
    zl, y, c = (lax.axis_index(a) for a in DP)
    piece = (c * 4 + y) * 4 + zl
    part = feats // 32
    place = jnp.stack([y, piece]).astype(jnp.int32)

    def to_inner(value):
        lead = value.shape[:-1]
        k = len(lead)
        split = value.reshape(*lead, 4, 4, 2, own)
        return split.transpose(*range(k), k + 1, k + 2, k, k + 3).reshape(*lead, rank)

    grads = out_grads.reshape(tokens, 8, cols).transpose(1, 0, 2)
    grads_all = lax.all_to_all(grads, CZ, 0, 0, tiled=True)
    inputs = layer_inputs.reshape(tokens, 2, 4, 4, part).transpose(1, 3, 0, 2, 4)
    inputs_all = lax.all_to_all(inputs.reshape(8, tokens, 4 * part), CZ, 0, 0, tiled=True)
    moments = jnp.stack([first, second]).reshape(2, own, 8, cols).transpose(2, 0, 1, 3)
    moments = lax.all_to_all(moments, CZ, 0, 0, tiled=True)
    moments = stack(moments, "y", True).reshape(4, 2, 4, 2, own, cols)

    basis_low = basis.astype(BF16)
    score_part = jnp.dot(layer_inputs, basis_low, preferred_element_type=F32)
    score_own = all_sum(scatter_near(score_part, "x"), "zh")
    scores = stack(to_inner(score_own.astype(BF16)), "x").reshape(tokens, rank)
    scores_all = stack(stack(scores, "zl"), "c").reshape(8 * tokens, rank)

    grad_part = low(scores_all, grads_all.reshape(8 * tokens, cols), TN)
    grad_own = scatter_sum(grad_part, "y")
    grad_low = stack_dp(grad_own.astype(BF16))
    back_part = back_product(grads.reshape(2, 4, tokens, cols), grad_low)
    back_own = all_sum(scatter_near(back_part, "x"), "zh")
    backward = stack(back_own.astype(BF16), "x").reshape(tokens, rank)
    backward_all = stack(stack(backward, "zl"), "c").reshape(8 * tokens, rank)
    tangent_part = low(inputs_all.reshape(8 * tokens, 4 * part), backward_all, TN)
    tangent = stack_dp(scatter_sum(tangent_part, "y"), True).reshape(feats, rank)

    basis_own = lax.dynamic_slice_in_dim(basis, piece * own, own, 1)
    tan_own = lax.dynamic_slice_in_dim(tangent, piece * own, own, 1)
    pair = jnp.concatenate(
        [exact(tan_own, tangent, TN), exact(tan_own, basis, TN), exact(basis_own, basis, TN)], axis=1
    )
    pair = sum_te(pair)
    pairs = stack_dp(pair, True).reshape(32, own, 3 * rank)
    vec, vec_own, rot_own, step, probe_part, scal = finish(
        place, pairs, tangent, basis, layer_inputs
    )
    new_basis = basis + jnp.outer(step[0], vec[0])
    probe = sum_te(probe_part)[0].astype(BF16)
    probe_all = lax.all_to_all(
        jnp.broadcast_to(probe[None], (8, tokens)), CZ, 0, 0, tiled=True
    ).reshape(8 * tokens)
    along_part = jnp.dot(probe_all, grads_all.reshape(8 * tokens, cols), preferred_element_type=F32)
    lead_part = jnp.sum(vec_own * grad_own, axis=0)
    push = all_sum(scal[0, 0] * lead_part + scal[0, 1] * along_part, "y")

    turned = turn(rot_own, moments)
    grad_new = grad_own + vec_own * push
    moved = jnp.stack(
        [0.9 * turned[0] + 0.1 * grad_new, 0.95 * turned[1] + 0.05 * grad_new * grad_new]
    )
    moved = moved.reshape(2, 8, own, cols).transpose(1, 0, 2, 3)
    moved = lax.all_to_all(moved, CZ, 0, 0, tiled=True)
    moved = moved.transpose(1, 2, 0, 3).reshape(2, own, 8 * cols)
    new_first, new_second = moved[0], moved[1]
    update = new_first / (jnp.sqrt(new_second) + 1e-06)
    return (new_basis, new_first, new_second, update)


def solution(mesh):
    fine = Mesh(mesh.devices.reshape(4, 4, 2, 2, 4), DP + TE)
    return jax.shard_map(
        body,
        mesh=fine,
        in_specs=(P(DP, TE), P(DP, TE), P(TE, None), P(DP, TE), P(DP, TE)),
        out_specs=(P(TE, None), P(DP, TE), P(DP, TE), P(DP, TE)),
        check_vma=False,
    )
```

```python
import jax
import jax.numpy as jnp
from jax import lax
from jax.experimental import pallas as pl
from jax.experimental.pallas import tpu as pltpu
from jax.sharding import Mesh, PartitionSpec as P

PI_STEPS = 6
EXACT = lax.Precision.HIGHEST
F32 = jnp.float32
BF16 = jnp.bfloat16
SIZES = {"zl": 4, "y": 4, "c": 2, "zh": 2, "x": 4}
DP = ("zl", "y", "c")
TE = ("zh", "x")


def shift(value, axis, k):
    n = SIZES[axis]
    return lax.ppermute(value, axis, [(i, (i - k) % n) for i in range(n)])


def all_sum(value, axis):
    if SIZES[axis] == 2:
        return value + shift(value, axis, 1)
    one, two, three = (shift(value, axis, k) for k in (1, 2, 3))
    return (value + two) + (one + three)


def scatter_sum(value, axis):
    n = SIZES[axis]
    moved = lax.all_to_all(value, axis, 0, 0, tiled=True)
    return moved.reshape(n, value.shape[0] // n, *value.shape[1:]).sum(0)


def scatter_near(value, axis):
    n = SIZES[axis]
    me = lax.axis_index(axis)
    rows = value.shape[0] // n

    def mine(k):
        return lax.dynamic_slice_in_dim(value, ((me + k) % n) * rows, rows, 0)

    one, two, three = (
        lax.ppermute(mine(k), axis, [(i, (i + k) % n) for i in range(n)]) for k in (1, 2, 3)
    )
    return (mine(0) + two) + (one + three)


def stack(value, axis, at_once=False):
    n = SIZES[axis]
    if at_once:
        many = jnp.broadcast_to(value[None], (n, *value.shape))
        return lax.all_to_all(many, axis, 0, 0, tiled=True)
    me = lax.axis_index(axis)
    if n == 2:
        other = shift(value, axis, 1)
        return jnp.where(me == 0, jnp.stack([value, other]), jnp.stack([other, value]))
    out = jnp.zeros((n, *value.shape), value.dtype)
    out = lax.dynamic_update_slice_in_dim(out, value[None], me, 0)
    for k in range(1, n):
        out = lax.dynamic_update_slice_in_dim(out, shift(value, axis, k)[None], (me + k) % n, 0)
    return out


def stack_dp(value, at_once=False):
    value = stack(value, "zl")
    value = stack(value, "y", at_once)
    return stack(value, "c")


def sum_te(value):
    return all_sum(all_sum(value, "zh"), "x")


NN, NT, TN = ((1,), (0,)), ((1,), (1,)), ((0,), (0,))


def exact(left, right, dims):
    return lax.dot_general(left, right, (dims, ((), ())), precision=EXACT, preferred_element_type=F32)


def low(left, right, dims):
    return lax.dot_general(left, right, (dims, ((), ())), preferred_element_type=F32)


def finish_kernel(
    place_ref, pairs_ref, tangent_ref, basis_ref, inputs_ref,
    vec_ref, own_ref, rot_ref, step_ref, probe_ref, scal_ref,
    kernel_ref, mixed_ref, col_ref,
):
    rank = kernel_ref.shape[0]
    own = rank // 32
    coup = pl.ds(rank, rank)
    wide = pl.ds(2 * rank, rank)

    half = rank // 2
    mixed_ref[...] = 2.0 * pairs_ref[:, :, coup].reshape(rank, rank)
    kernel_ref[...] = pairs_ref[:, :, pl.ds(0, rank)].reshape(rank, rank)

    def mix(i, carry):
        k, n = i // 2, i % 2
        out = pl.ds(pl.multiple_of(n * half, half), half)
        mixed_ref[:, out] -= exact(
            pairs_ref[:, :, pl.ds(pl.multiple_of(rank + k * half, half), half)].reshape(rank, half),
            pairs_ref[
                pl.ds(k * 16, 16), :, pl.ds(pl.multiple_of(2 * rank + n * half, half), half)
            ].reshape(half, half),
            NN,
        )
        return carry

    def fill(i, carry):
        k, n = i // 2, i % 2
        out = pl.ds(pl.multiple_of(n * half, half), half)
        kernel_ref[:, out] -= exact(
            mixed_ref[:, pl.ds(pl.multiple_of(k * half, half), half)],
            pairs_ref[
                pl.ds(n * 16, 16), :, pl.ds(pl.multiple_of(rank + k * half, half), half)
            ].reshape(half, half),
            NT,
        )
        return carry

    lax.fori_loop(0, 4, mix, 0)
    lax.fori_loop(0, 4, fill, 0)
    rows = lax.broadcasted_iota(jnp.int32, (rank, rank), 0)
    lanes = lax.broadcasted_iota(jnp.int32, (rank, rank), 1)
    total = jnp.sum(jnp.where(rows == lanes, kernel_ref[...], 0.0), keepdims=True)
    inv = 1.0 / total

    def to_row(col):
        return jnp.sum(kernel_ref[...] * col, axis=0, keepdims=True) * inv

    def to_col(row):
        return jnp.sum(kernel_ref[...] * row, axis=1, keepdims=True) * inv

    def unit(vec):
        return vec / jnp.sqrt(jnp.sum(vec * vec, keepdims=True) + 1e-12)

    col_ref[...] = jnp.full((rank, 1), 1.0, F32) / jnp.sqrt(F32(rank))

    def sweep(i, carry):
        col_ref[...] = unit(to_col(unit(to_row(col_ref[...]))))
        return carry

    lax.fori_loop(0, PI_STEPS // 2, sweep, 0)
    col = col_ref[...]
    last = to_row(col)
    row = jnp.sum(jnp.where(rows == lanes, col, 0.0), axis=0, keepdims=True)
    ratio = jnp.sum(row * last, keepdims=True)
    group = lanes // own
    source = ((group // 2) % 4) * 8 + (group % 2) * 4 + group // 8
    vector = jnp.sum(jnp.where(rows == source * own + lanes % own, col, 0.0), axis=0, keepdims=True)
    theta = 4.0 * jnp.sqrt(ratio)
    sigma = jnp.sqrt(total * ratio + 1e-06)
    shrink = jnp.cos(theta) - 1.0
    sine = jnp.sin(theta)

    def tall(vec):
        return jnp.broadcast_to(vec, (8, vec.shape[1]))

    coup_vec = exact(tall(row), pairs_ref[:, :, coup].reshape(rank, rank), NN)
    both = exact(
        jnp.concatenate([tall(vector), coup_vec], axis=0), pairs_ref[:, :, wide].reshape(rank, rank), NN
    )
    tail = (shrink * both[:8] + (sine / sigma) * (coup_vec - both[8:]))[:1]
    turned = exact(jnp.concatenate([coup_vec, tall(vector)], axis=0), basis_ref[...], NT)
    left = (exact(tall(row), tangent_ref[...], NT) - turned[:8]) / sigma
    probe_ref[...] = low(left.astype(BF16), inputs_ref[...], NT)
    vec_ref[...] = tall(vector)
    step_ref[...] = shrink * turned[8:] + sine * left
    lane = lax.broadcasted_iota(jnp.int32, scal_ref.shape, 1)
    scal_ref[...] = jnp.where(lane == 0, shrink, sine)
    y = place_ref[0]
    own_ref[...] = col_ref[pl.ds(pl.multiple_of(y * 8 * own, 8 * own), 8 * own), :]
    for c in range(2):
        for zl in range(4):
            some = pl.ds((c * 4 + zl) * own, own)
            rot_ref[some, :] = pairs_ref[zl * 8 + y * 2 + c, :, wide] + own_ref[some, :] * tail


def finish(place, pairs, tangent, basis, inputs):
    rank = basis.shape[1]
    vmem = pl.BlockSpec(memory_space=pltpu.VMEM)
    return pl.pallas_call(
        finish_kernel,
        out_shape=(
            jax.ShapeDtypeStruct((8, rank), F32),
            jax.ShapeDtypeStruct((rank // 4, 1), F32),
            jax.ShapeDtypeStruct((rank // 4, rank), F32),
            jax.ShapeDtypeStruct((8, tangent.shape[0]), F32),
            jax.ShapeDtypeStruct((8, inputs.shape[0]), F32),
            jax.ShapeDtypeStruct((8, 128), F32),
        ),
        in_specs=[pl.BlockSpec(memory_space=pltpu.SMEM)] + [vmem] * 4,
        out_specs=(vmem,) * 6,
        scratch_shapes=[pltpu.VMEM((rank, rank), F32)] * 2 + [pltpu.VMEM((rank, 1), F32)],
        compiler_params=pltpu.CompilerParams(vmem_limit_bytes=40 * 1024 * 1024),
    )(place, pairs, tangent, basis, inputs)


def turn_kernel(rot_ref, moments_ref, out_ref):
    for which in range(2):
        rows = jnp.concatenate(
            [
                moments_ref[y, c, zl, which]
                for zl in range(4)
                for y in range(4)
                for c in range(2)
            ],
            axis=0,
        )
        rot = rot_ref[...]
        out_ref[which] = exact(rot if which == 0 else rot * rot, rows, NN)


def turn(rot, moments):
    cols = moments.shape[-1]
    vmem = pl.BlockSpec(memory_space=pltpu.VMEM)
    return pl.pallas_call(
        turn_kernel,
        out_shape=jax.ShapeDtypeStruct((2, rot.shape[0], cols), F32),
        in_specs=[vmem] * 2,
        out_specs=vmem,
        compiler_params=pltpu.CompilerParams(vmem_limit_bytes=24 * 1024 * 1024),
    )(rot, moments)


def back_kernel(grads_ref, low_ref, out_ref):
    rows, cols = low_ref.shape[3:]
    for c in range(2):
        for zl in range(4):
            start = (c * 4 + zl) * cols
            block = grads_ref[:, start : start + cols]
            for y in range(4):
                part = low(block, low_ref[c, y, zl], NT)
                if c + zl > 0:
                    part += out_ref[:, y * rows : (y + 1) * rows]
                out_ref[:, y * rows : (y + 1) * rows] = part


def back_product(grads, low_rows):
    tokens = grads.shape[0]
    vmem = pl.BlockSpec(memory_space=pltpu.VMEM)
    return pl.pallas_call(
        back_kernel,
        out_shape=jax.ShapeDtypeStruct((tokens, 4 * low_rows.shape[3]), F32),
        in_specs=[vmem] * 2,
        out_specs=vmem,
        compiler_params=pltpu.CompilerParams(vmem_limit_bytes=24 * 1024 * 1024),
    )(grads, low_rows)


CZ = ("c", "zl")


def body(layer_inputs, out_grads, basis, first, second):
    tokens, feats = layer_inputs.shape
    cols = out_grads.shape[1] // 8
    rank = basis.shape[1]
    own = rank // 32
    zl, y, c = (lax.axis_index(a) for a in DP)
    piece = (c * 4 + y) * 4 + zl
    part = feats // 32
    place = jnp.stack([y, piece]).astype(jnp.int32)

    def to_inner(value):
        lead = value.shape[:-1]
        k = len(lead)
        split = value.reshape(*lead, 4, 4, 2, own)
        return split.transpose(*range(k), k + 1, k + 2, k, k + 3).reshape(*lead, rank)

    grads = out_grads.reshape(tokens, 8, cols).transpose(1, 0, 2)
    grads_all = lax.all_to_all(grads, CZ, 0, 0, tiled=True)
    inputs = layer_inputs.reshape(tokens, 2, 4, 4, part).transpose(1, 3, 0, 2, 4)
    inputs_all = lax.all_to_all(inputs.reshape(8, tokens, 4 * part), CZ, 0, 0, tiled=True)
    moments = jnp.stack([first, second]).reshape(2, own, 8, cols).transpose(2, 0, 1, 3)
    moments = lax.all_to_all(moments, CZ, 0, 0, tiled=True)
    moments = stack(moments, "y", True).reshape(4, 2, 4, 2, own, cols)

    basis_low = basis.astype(BF16)
    score_part = jnp.dot(layer_inputs, basis_low, preferred_element_type=F32)
    score_own = scatter_near(score_part, "x")
    score_own = all_sum(score_own, "zh")
    scores = stack(to_inner(score_own.astype(BF16)), "x").reshape(tokens, rank)
    scores_all = stack(stack(scores, "zl"), "c").reshape(8 * tokens, rank)

    grad_part = low(scores_all, grads_all.reshape(8 * tokens, cols), TN)
    grad_own = scatter_sum(grad_part, "y")
    grad_low = stack_dp(grad_own.astype(BF16))
    back_part = back_product(out_grads, grad_low)
    back_own = scatter_near(back_part, "x")
    back_own = all_sum(back_own, "zh")
    backward = stack(back_own.astype(BF16), "x").reshape(tokens, rank)
    backward_all = stack(stack(backward, "zl"), "c").reshape(8 * tokens, rank)
    tangent_part = low(inputs_all.reshape(8 * tokens, 4 * part), backward_all, TN)
    tangent = stack_dp(scatter_sum(tangent_part, "y"), True).reshape(feats, rank)

    basis_own = lax.dynamic_slice_in_dim(basis, piece * own, own, 1)
    tan_own = lax.dynamic_slice_in_dim(tangent, piece * own, own, 1)
    pair = jnp.concatenate(
        [exact(tan_own, tangent, TN), exact(tan_own, basis, TN), exact(basis_own, basis, TN)], axis=1
    )
    pair = sum_te(pair)
    pairs = stack_dp(pair, True).reshape(32, own, 3 * rank)
    vec, vec_own, rot_own, step, probe_part, scal = finish(
        place, pairs, tangent, basis, layer_inputs
    )
    new_basis = basis + jnp.outer(step[0], vec[0])
    probe_many = jnp.broadcast_to(probe_part[:1], (8, tokens))
    probe = lax.all_to_all(probe_many, TE, 0, 0, tiled=True).sum(0).astype(BF16)
    along_part = jnp.dot(probe, out_grads, preferred_element_type=F32).reshape(2, 4, cols)
    lead_part = jnp.sum(vec_own * grad_own, axis=0)
    mine = (jnp.arange(2)[:, None] == c) & (jnp.arange(4)[None] == zl)
    push_part = scal[0, 1] * along_part + jnp.where(mine[:, :, None], scal[0, 0] * lead_part, 0.0)
    push_many = jnp.broadcast_to(push_part.transpose(1, 0, 2)[:, None], (4, 4, 2, cols))
    push = lax.all_to_all(push_many.reshape(32, cols), DP, 0, 0, tiled=True).sum(0)

    turned = turn(rot_own, moments)
    grad_new = grad_own + vec_own * push
    moved = jnp.stack(
        [0.9 * turned[0] + 0.1 * grad_new, 0.95 * turned[1] + 0.05 * grad_new * grad_new]
    )
    moved = moved.reshape(2, 8, own, cols).transpose(1, 0, 2, 3)
    moved = lax.all_to_all(moved, CZ, 0, 0, tiled=True)
    moved = moved.transpose(1, 2, 0, 3).reshape(2, own, 8 * cols)
    new_first, new_second = moved[0], moved[1]
    update = new_first / (jnp.sqrt(new_second) + 1e-06)
    return (new_basis, new_first, new_second, update)


def solution(mesh):
    fine = Mesh(mesh.devices.reshape(4, 4, 2, 2, 4), DP + TE)
    return jax.shard_map(
        body,
        mesh=fine,
        in_specs=(P(DP, TE), P(DP, TE), P(TE, None), P(DP, TE), P(DP, TE)),
        out_specs=(P(TE, None), P(DP, TE), P(DP, TE), P(DP, TE)),
        check_vma=False,
    )
```

```python
import jax
import jax.numpy as jnp
from jax import lax
from jax.experimental import pallas as pl
from jax.experimental.pallas import tpu as pltpu
from jax.sharding import Mesh, PartitionSpec as P

PI_STEPS = 6
EXACT = lax.Precision.HIGHEST
F32 = jnp.float32
BF16 = jnp.bfloat16
SIZES = {"zl": 4, "y": 4, "c": 2, "zh": 2, "x": 4}
DP = ("zl", "y", "c")
TE = ("zh", "x")


def shift(value, axis, k):
    n = SIZES[axis]
    return lax.ppermute(value, axis, [(i, (i - k) % n) for i in range(n)])


def all_sum(value, axis):
    if SIZES[axis] == 2:
        return value + shift(value, axis, 1)
    one, two, three = (shift(value, axis, k) for k in (1, 2, 3))
    return (value + two) + (one + three)


def scatter_sum(value, axis):
    n = SIZES[axis]
    moved = lax.all_to_all(value, axis, 0, 0, tiled=True)
    return moved.reshape(n, value.shape[0] // n, *value.shape[1:]).sum(0)


def scatter_near(value, axis):
    n = SIZES[axis]
    me = lax.axis_index(axis)
    rows = value.shape[0] // n

    def mine(k):
        return lax.dynamic_slice_in_dim(value, ((me + k) % n) * rows, rows, 0)

    one, two, three = (
        lax.ppermute(mine(k), axis, [(i, (i + k) % n) for i in range(n)]) for k in (1, 2, 3)
    )
    return (mine(0) + two) + (one + three)


def stack(value, axis, at_once=False):
    n = SIZES[axis]
    if at_once:
        many = jnp.broadcast_to(value[None], (n, *value.shape))
        return lax.all_to_all(many, axis, 0, 0, tiled=True)
    me = lax.axis_index(axis)
    if n == 2:
        other = shift(value, axis, 1)
        return jnp.where(me == 0, jnp.stack([value, other]), jnp.stack([other, value]))
    out = jnp.zeros((n, *value.shape), value.dtype)
    out = lax.dynamic_update_slice_in_dim(out, value[None], me, 0)
    for k in range(1, n):
        out = lax.dynamic_update_slice_in_dim(out, shift(value, axis, k)[None], (me + k) % n, 0)
    return out


def stack_yz(value, at_once=False):
    value = stack(value, "zl")
    return stack(value, "y", at_once)


def sum_te(value):
    return all_sum(all_sum(value, "zh"), "x")


NN, NT, TN = ((1,), (0,)), ((1,), (1,)), ((0,), (0,))


def exact(left, right, dims):
    return lax.dot_general(left, right, (dims, ((), ())), precision=EXACT, preferred_element_type=F32)


def low(left, right, dims):
    return lax.dot_general(left, right, (dims, ((), ())), preferred_element_type=F32)


def finish_kernel(
    place_ref, pairs_ref, tangent_ref, basis_ref, inputs_ref,
    vec_ref, own_ref, rot_ref, step_ref, probe_ref, scal_ref,
    kernel_ref, mixed_ref, col_ref,
):
    rank = kernel_ref.shape[0]
    own = rank // 32
    coup = pl.ds(rank, rank)
    wide = pl.ds(2 * rank, rank)

    half = rank // 2
    mixed_ref[...] = 2.0 * pairs_ref[:, :, coup].reshape(rank, rank)
    kernel_ref[...] = pairs_ref[:, :, pl.ds(0, rank)].reshape(rank, rank)

    def mix(i, carry):
        k, n = i // 2, i % 2
        out = pl.ds(pl.multiple_of(n * half, half), half)
        mixed_ref[:, out] -= exact(
            pairs_ref[:, :, pl.ds(pl.multiple_of(rank + k * half, half), half)].reshape(rank, half),
            pairs_ref[
                pl.ds(k * 16, 16), :, pl.ds(pl.multiple_of(2 * rank + n * half, half), half)
            ].reshape(half, half),
            NN,
        )
        return carry

    def fill(i, carry):
        k, n = i // 2, i % 2
        out = pl.ds(pl.multiple_of(n * half, half), half)
        kernel_ref[:, out] -= exact(
            mixed_ref[:, pl.ds(pl.multiple_of(k * half, half), half)],
            pairs_ref[
                pl.ds(n * 16, 16), :, pl.ds(pl.multiple_of(rank + k * half, half), half)
            ].reshape(half, half),
            NT,
        )
        return carry

    lax.fori_loop(0, 4, mix, 0)
    lax.fori_loop(0, 4, fill, 0)
    rows = lax.broadcasted_iota(jnp.int32, (rank, rank), 0)
    lanes = lax.broadcasted_iota(jnp.int32, (rank, rank), 1)
    total = jnp.sum(jnp.where(rows == lanes, kernel_ref[...], 0.0), keepdims=True)
    inv = 1.0 / total

    def to_row(col):
        return jnp.sum(kernel_ref[...] * col, axis=0, keepdims=True) * inv

    def to_col(row):
        return jnp.sum(kernel_ref[...] * row, axis=1, keepdims=True) * inv

    def unit(vec):
        return vec / jnp.sqrt(jnp.sum(vec * vec, keepdims=True) + 1e-12)

    col_ref[...] = jnp.full((rank, 1), 1.0, F32) / jnp.sqrt(F32(rank))

    def sweep(i, carry):
        col_ref[...] = unit(to_col(unit(to_row(col_ref[...]))))
        return carry

    lax.fori_loop(0, PI_STEPS // 2, sweep, 0)
    col = col_ref[...]
    last = to_row(col)
    row = jnp.sum(jnp.where(rows == lanes, col, 0.0), axis=0, keepdims=True)
    ratio = jnp.sum(row * last, keepdims=True)
    group = lanes // own
    source = ((group // 2) % 4) * 8 + (group % 2) * 4 + group // 8
    vector = jnp.sum(jnp.where(rows == source * own + lanes % own, col, 0.0), axis=0, keepdims=True)
    theta = 4.0 * jnp.sqrt(ratio)
    sigma = jnp.sqrt(total * ratio + 1e-06)
    shrink = jnp.cos(theta) - 1.0
    sine = jnp.sin(theta)

    coup_row = jnp.sum(pairs_ref[:, :, coup].reshape(rank, rank) * col, axis=0, keepdims=True)
    gram = pairs_ref[:, :, wide].reshape(rank, rank)

    def flip(vec):
        return jnp.sum(jnp.where(rows == lanes, vec, 0.0), axis=1, keepdims=True)

    tail = shrink * jnp.sum(gram * flip(vector), axis=0, keepdims=True) + (sine / sigma) * (
        coup_row - jnp.sum(gram * flip(coup_row), axis=0, keepdims=True)
    )
    size = inputs_ref.shape[0]
    feats = basis_ref.shape[0]

    def rise(i, carry):
        some = pl.ds(pl.multiple_of(i * size, size), size)
        old = basis_ref[some, :]
        left = jnp.sum(tangent_ref[some, :] * row - old * coup_row, axis=1, keepdims=True) / sigma
        step_ref[some, :] = shrink * jnp.sum(old * vector, axis=1, keepdims=True) + sine * left
        wide_left = jnp.broadcast_to(left, (size, size)).astype(BF16)
        return carry + low(inputs_ref[:, some], wide_left, NN)

    probe = lax.fori_loop(0, feats // size, rise, jnp.zeros((size, size), F32))
    spots = lax.broadcasted_iota(jnp.int32, (size, size), 0) == lax.broadcasted_iota(
        jnp.int32, (size, size), 1
    )
    probe_ref[...] = jnp.broadcast_to(
        jnp.sum(jnp.where(spots, probe, 0.0), axis=0, keepdims=True), probe_ref.shape
    )
    vec_ref[...] = jnp.broadcast_to(vector, vec_ref.shape)
    lane = lax.broadcasted_iota(jnp.int32, scal_ref.shape, 1)
    scal_ref[...] = jnp.where(lane == 0, shrink, sine)
    y = place_ref[0]
    own_ref[...] = col_ref[pl.ds(pl.multiple_of(y * 8 * own, 8 * own), 8 * own), :]
    for c in range(2):
        for zl in range(4):
            some = pl.ds((c * 4 + zl) * own, own)
            rot_ref[some, :] = pairs_ref[zl * 8 + y * 2 + c, :, wide] + own_ref[some, :] * tail


def finish(place, pairs, tangent, basis, inputs):
    rank = basis.shape[1]
    vmem = pl.BlockSpec(memory_space=pltpu.VMEM)
    return pl.pallas_call(
        finish_kernel,
        out_shape=(
            jax.ShapeDtypeStruct((8, rank), F32),
            jax.ShapeDtypeStruct((rank // 4, 1), F32),
            jax.ShapeDtypeStruct((rank // 4, rank), F32),
            jax.ShapeDtypeStruct((tangent.shape[0], 1), F32),
            jax.ShapeDtypeStruct((8, inputs.shape[0]), F32),
            jax.ShapeDtypeStruct((8, 128), F32),
        ),
        in_specs=[pl.BlockSpec(memory_space=pltpu.SMEM)] + [vmem] * 4,
        out_specs=(vmem,) * 6,
        scratch_shapes=[pltpu.VMEM((rank, rank), F32)] * 2 + [pltpu.VMEM((rank, 1), F32)],
        compiler_params=pltpu.CompilerParams(vmem_limit_bytes=40 * 1024 * 1024),
    )(place, pairs, tangent, basis, inputs)


def turn_kernel(rot_ref, moments_ref, out_ref):
    for which in range(2):
        rows = jnp.concatenate(
            [
                moments_ref[y, c, zl, which]
                for zl in range(4)
                for y in range(4)
                for c in range(2)
            ],
            axis=0,
        )
        rot = rot_ref[...]
        out_ref[which] = exact(rot if which == 0 else rot * rot, rows, NN)


def turn(rot, moments):
    cols = moments.shape[-1]
    vmem = pl.BlockSpec(memory_space=pltpu.VMEM)
    return pl.pallas_call(
        turn_kernel,
        out_shape=jax.ShapeDtypeStruct((2, rot.shape[0], cols), F32),
        in_specs=[vmem] * 2,
        out_specs=vmem,
        compiler_params=pltpu.CompilerParams(vmem_limit_bytes=24 * 1024 * 1024),
    )(rot, moments)


def back_kernel(place_ref, grads_ref, mine_ref, other_ref, out_ref):
    rows, cols = mine_ref.shape[2:]
    for half, low_ref in enumerate((mine_ref, other_ref)):
        c = place_ref[2] if half == 0 else 1 - place_ref[2]
        wide = grads_ref[:, pl.ds(pl.multiple_of(c * 4 * cols, 128), 4 * cols)]
        for zl in range(4):
            block = wide[:, zl * cols : (zl + 1) * cols]
            for y in range(4):
                part = low(block, low_ref[y, zl], NT)
                if half + zl > 0:
                    part += out_ref[:, y * rows : (y + 1) * rows]
                out_ref[:, y * rows : (y + 1) * rows] = part


def back_product(place, grads, mine, other):
    tokens = grads.shape[0]
    vmem = pl.BlockSpec(memory_space=pltpu.VMEM)
    return pl.pallas_call(
        back_kernel,
        out_shape=jax.ShapeDtypeStruct((tokens, 4 * mine.shape[2]), F32),
        in_specs=[pl.BlockSpec(memory_space=pltpu.SMEM)] + [vmem] * 3,
        out_specs=vmem,
        compiler_params=pltpu.CompilerParams(vmem_limit_bytes=24 * 1024 * 1024),
    )(place, grads, mine, other)


def pair_kernel(place_ref, mine_ref, other_ref, basis_ref, tangent_ref, out_ref, total_ref):
    half, rank = mine_ref.shape
    own = out_ref.shape[0]
    c = place_ref[2]
    tangent_ref[pl.ds(pl.multiple_of(c * half, half), half), :] = mine_ref[...]
    tangent_ref[pl.ds(pl.multiple_of((1 - c) * half, half), half), :] = other_ref[...]
    start = pl.multiple_of((place_ref[1] // 8) * 128, 128)
    spot = pl.multiple_of((place_ref[1] % 8) * own, own)
    total_ref[...] = jnp.zeros_like(total_ref)

    def step(k, carry):
        some = pl.ds(pl.multiple_of(k * 256, 256), 256)
        tan = tangent_ref[some, pl.ds(start, 128)]
        bas = basis_ref[some, pl.ds(start, 128)]
        total_ref[:, pl.ds(0, rank)] += exact(tan, tangent_ref[some, :], TN)
        total_ref[:, pl.ds(rank, rank)] += exact(tan, basis_ref[some, :], TN)
        total_ref[:, pl.ds(2 * rank, rank)] += exact(bas, basis_ref[some, :], TN)
        return carry

    lax.fori_loop(0, 2 * half // 256, step, 0)
    out_ref[...] = total_ref[pl.ds(spot, own), :]


def pair_products(place, mine, other, basis):
    rank = basis.shape[1]
    vmem = pl.BlockSpec(memory_space=pltpu.VMEM)
    return pl.pallas_call(
        pair_kernel,
        out_shape=(
            jax.ShapeDtypeStruct(basis.shape, F32),
            jax.ShapeDtypeStruct((rank // 32, 3 * rank), F32),
        ),
        in_specs=[pl.BlockSpec(memory_space=pltpu.SMEM)] + [vmem] * 3,
        out_specs=(vmem,) * 2,
        scratch_shapes=[pltpu.VMEM((128, 3 * rank), F32)],
        compiler_params=pltpu.CompilerParams(vmem_limit_bytes=24 * 1024 * 1024),
    )(place, mine, other, basis)


CZ = ("c", "zl")


def body(layer_inputs, out_grads, basis, first, second):
    tokens, feats = layer_inputs.shape
    cols = out_grads.shape[1] // 8
    rank = basis.shape[1]
    own = rank // 32
    zl, y, c = (lax.axis_index(a) for a in DP)
    piece = (c * 4 + y) * 4 + zl
    part = feats // 32
    place = jnp.stack([y, piece, c]).astype(jnp.int32)

    def to_inner(value):
        lead = value.shape[:-1]
        k = len(lead)
        split = value.reshape(*lead, 4, 4, 2, own)
        return split.transpose(*range(k), k + 1, k + 2, k, k + 3).reshape(*lead, rank)

    grads = out_grads.reshape(tokens, 8, cols).transpose(1, 0, 2)
    grads_all = lax.all_to_all(grads, CZ, 0, 0, tiled=True)
    inputs = layer_inputs.reshape(tokens, 2, 4, 4, part).transpose(1, 3, 0, 2, 4)
    inputs_all = lax.all_to_all(inputs.reshape(8, tokens, 4 * part), CZ, 0, 0, tiled=True)
    moments = jnp.stack([first, second]).reshape(2, own, 8, cols).transpose(2, 0, 1, 3)
    moments = lax.all_to_all(moments, CZ, 0, 0, tiled=True)
    moments = stack(moments, "y", True).reshape(4, 2, 4, 2, own, cols)

    basis_low = basis.astype(BF16)
    score_part = jnp.dot(layer_inputs, basis_low, preferred_element_type=F32)
    score_own = scatter_near(score_part, "x")
    score_own = all_sum(score_own, "zh")
    scores = stack(to_inner(score_own.astype(BF16)), "x").reshape(tokens, rank)
    scores_all = stack(stack(scores, "zl"), "c").reshape(8 * tokens, rank)

    grad_part = low(scores_all, grads_all.reshape(8 * tokens, cols), TN)
    grad_own = scatter_sum(grad_part, "y")
    grad_low = stack_yz(grad_own.astype(BF16))
    grad_far = shift(grad_low, "c", 1)
    back_part = back_product(place, out_grads, grad_low, grad_far)
    back_own = scatter_near(back_part, "x")
    back_own = all_sum(back_own, "zh")
    backward = stack(back_own.astype(BF16), "x").reshape(tokens, rank)
    backward_all = stack(stack(backward, "zl"), "c").reshape(8 * tokens, rank)
    tangent_part = low(inputs_all.reshape(8 * tokens, 4 * part), backward_all, TN)
    tan_near = stack_yz(scatter_sum(tangent_part, "y"), True).reshape(feats // 2, rank)
    tan_far = shift(tan_near, "c", 1)

    tangent, pair = pair_products(place, tan_near, tan_far, basis)
    pair = sum_te(pair)
    pairs = stack(stack_yz(pair, True), "c").reshape(32, own, 3 * rank)
    vec, vec_own, rot_own, step, probe_part, scal = finish(
        place, pairs, tangent, basis, layer_inputs
    )
    new_basis = basis + step * vec[:1]
    probe = sum_te(probe_part)[0].astype(BF16)
    along_part = jnp.dot(probe, out_grads, preferred_element_type=F32).reshape(2, 4, cols)
    lead_part = jnp.sum(vec_own * grad_own, axis=0)
    mine = (jnp.arange(2)[:, None] == c) & (jnp.arange(4)[None] == zl)
    push_part = scal[0, 1] * along_part + jnp.where(mine[:, :, None], scal[0, 0] * lead_part, 0.0)
    push_many = jnp.broadcast_to(push_part.transpose(1, 0, 2)[:, None], (4, 4, 2, cols))
    push = lax.all_to_all(push_many.reshape(32, cols), DP, 0, 0, tiled=True).sum(0)

    turned = turn(rot_own, moments)
    grad_new = grad_own + vec_own * push
    moved = jnp.stack(
        [0.9 * turned[0] + 0.1 * grad_new, 0.95 * turned[1] + 0.05 * grad_new * grad_new]
    )
    moved = moved.reshape(2, 8, own, cols).transpose(1, 0, 2, 3)
    moved = lax.all_to_all(moved, CZ, 0, 0, tiled=True)
    moved = moved.transpose(1, 2, 0, 3).reshape(2, own, 8 * cols)
    new_first, new_second = moved[0], moved[1]
    update = new_first / (jnp.sqrt(new_second) + 1e-06)
    return (new_basis, new_first, new_second, update)


def solution(mesh):
    fine = Mesh(mesh.devices.reshape(4, 4, 2, 2, 4), DP + TE)
    return jax.shard_map(
        body,
        mesh=fine,
        in_specs=(P(DP, TE), P(DP, TE), P(TE, None), P(DP, TE), P(DP, TE)),
        out_specs=(P(TE, None), P(DP, TE), P(DP, TE), P(DP, TE)),
        check_vma=False,
    )
```

```python
import jax
import jax.numpy as jnp
from jax import lax
from jax.experimental import pallas as pl
from jax.experimental.pallas import tpu as pltpu
from jax.sharding import Mesh, PartitionSpec as P

PI_STEPS = 6
EXACT = lax.Precision.HIGHEST
F32 = jnp.float32
BF16 = jnp.bfloat16
SIZES = {"zl": 4, "y": 4, "c": 2, "zh": 2, "x": 4}
DP = ("zl", "y", "c")
TE = ("zh", "x")


def shift(value, axis, k):
    n = SIZES[axis]
    return lax.ppermute(value, axis, [(i, (i - k) % n) for i in range(n)])


def all_sum(value, axis):
    if SIZES[axis] == 2:
        return value + shift(value, axis, 1)
    one, two, three = (shift(value, axis, k) for k in (1, 2, 3))
    return (value + two) + (one + three)


def scatter_sum(value, axis):
    n = SIZES[axis]
    moved = lax.all_to_all(value, axis, 0, 0, tiled=True)
    return moved.reshape(n, value.shape[0] // n, *value.shape[1:]).sum(0)


def scatter_near(value, axis):
    n = SIZES[axis]
    me = lax.axis_index(axis)
    rows = value.shape[0] // n

    def mine(k):
        return lax.dynamic_slice_in_dim(value, ((me + k) % n) * rows, rows, 0)

    one, two, three = (
        lax.ppermute(mine(k), axis, [(i, (i + k) % n) for i in range(n)]) for k in (1, 2, 3)
    )
    return (mine(0) + two) + (one + three)


def stack(value, axis, at_once=False):
    n = SIZES[axis]
    if at_once:
        many = jnp.broadcast_to(value[None], (n, *value.shape))
        return lax.all_to_all(many, axis, 0, 0, tiled=True)
    me = lax.axis_index(axis)
    if n == 2:
        other = shift(value, axis, 1)
        return jnp.where(me == 0, jnp.stack([value, other]), jnp.stack([other, value]))
    out = jnp.zeros((n, *value.shape), value.dtype)
    out = lax.dynamic_update_slice_in_dim(out, value[None], me, 0)
    for k in range(1, n):
        out = lax.dynamic_update_slice_in_dim(out, shift(value, axis, k)[None], (me + k) % n, 0)
    return out


def stack_yz(value, at_once=False):
    value = stack(value, "zl", True)
    return stack(value, "y", at_once)


NN, NT, TN = ((1,), (0,)), ((1,), (1,)), ((0,), (0,))


def exact(left, right, dims):
    return lax.dot_general(left, right, (dims, ((), ())), precision=EXACT, preferred_element_type=F32)


def low(left, right, dims):
    return lax.dot_general(left, right, (dims, ((), ())), preferred_element_type=F32)


def finish_kernel(
    place_ref, pairs_ref, tangent_ref, basis_ref, inputs_ref,
    vec_ref, own_ref, rot_ref, step_ref, probe_ref, scal_ref,
    kernel_ref, mixed_ref, col_ref,
):
    rank = kernel_ref.shape[0]
    own = rank // 32
    coup = pl.ds(rank, rank)
    wide = pl.ds(2 * rank, rank)

    half = rank // 2
    mixed_ref[...] = 2.0 * pairs_ref[:, :, coup].reshape(rank, rank)
    kernel_ref[...] = pairs_ref[:, :, pl.ds(0, rank)].reshape(rank, rank)

    def mix(i, carry):
        k, n = i // 2, i % 2
        out = pl.ds(pl.multiple_of(n * half, half), half)
        mixed_ref[:, out] -= exact(
            pairs_ref[:, :, pl.ds(pl.multiple_of(rank + k * half, half), half)].reshape(rank, half),
            pairs_ref[
                pl.ds(k * 16, 16), :, pl.ds(pl.multiple_of(2 * rank + n * half, half), half)
            ].reshape(half, half),
            NN,
        )
        return carry

    def fill(i, carry):
        k, n = i // 2, i % 2
        out = pl.ds(pl.multiple_of(n * half, half), half)
        kernel_ref[:, out] -= exact(
            mixed_ref[:, pl.ds(pl.multiple_of(k * half, half), half)],
            pairs_ref[
                pl.ds(n * 16, 16), :, pl.ds(pl.multiple_of(rank + k * half, half), half)
            ].reshape(half, half),
            NT,
        )
        return carry

    lax.fori_loop(0, 4, mix, 0)
    lax.fori_loop(0, 4, fill, 0)
    rows = lax.broadcasted_iota(jnp.int32, (rank, rank), 0)
    lanes = lax.broadcasted_iota(jnp.int32, (rank, rank), 1)
    total = jnp.sum(jnp.where(rows == lanes, kernel_ref[...], 0.0), keepdims=True)
    inv = 1.0 / total

    def to_row(col):
        return jnp.sum(kernel_ref[...] * col, axis=0, keepdims=True) * inv

    def to_col(row):
        return jnp.sum(kernel_ref[...] * row, axis=1, keepdims=True) * inv

    def unit(vec):
        return vec / jnp.sqrt(jnp.sum(vec * vec, keepdims=True) + 1e-12)

    col_ref[...] = jnp.full((rank, 1), 1.0, F32) / jnp.sqrt(F32(rank))

    def sweep(i, carry):
        col_ref[...] = unit(to_col(unit(to_row(col_ref[...]))))
        return carry

    lax.fori_loop(0, PI_STEPS // 2, sweep, 0)
    col = col_ref[...]
    last = to_row(col)
    row = jnp.sum(jnp.where(rows == lanes, col, 0.0), axis=0, keepdims=True)
    ratio = jnp.sum(row * last, keepdims=True)
    group = lanes // own
    source = ((group // 2) % 4) * 8 + (group % 2) * 4 + group // 8
    vector = jnp.sum(jnp.where(rows == source * own + lanes % own, col, 0.0), axis=0, keepdims=True)
    theta = 4.0 * jnp.sqrt(ratio)
    sigma = jnp.sqrt(total * ratio + 1e-06)
    shrink = jnp.cos(theta) - 1.0
    sine = jnp.sin(theta)

    coup_row = jnp.sum(pairs_ref[:, :, coup].reshape(rank, rank) * col, axis=0, keepdims=True)
    gram = pairs_ref[:, :, wide].reshape(rank, rank)

    def flip(vec):
        return jnp.sum(jnp.where(rows == lanes, vec, 0.0), axis=1, keepdims=True)

    tail = shrink * jnp.sum(gram * flip(vector), axis=0, keepdims=True) + (sine / sigma) * (
        coup_row - jnp.sum(gram * flip(coup_row), axis=0, keepdims=True)
    )
    size = inputs_ref.shape[0]
    feats = basis_ref.shape[0]

    def rise(i, carry):
        some = pl.ds(pl.multiple_of(i * size, size), size)
        old = basis_ref[some, :]
        left = jnp.sum(tangent_ref[some, :] * row - old * coup_row, axis=1, keepdims=True) / sigma
        step_ref[some, :] = shrink * jnp.sum(old * vector, axis=1, keepdims=True) + sine * left
        wide_left = jnp.broadcast_to(left, (size, size)).astype(BF16)
        return carry + low(inputs_ref[:, some], wide_left, NN)

    probe = lax.fori_loop(0, feats // size, rise, jnp.zeros((size, size), F32))
    spots = lax.broadcasted_iota(jnp.int32, (size, size), 0) == lax.broadcasted_iota(
        jnp.int32, (size, size), 1
    )
    probe_ref[...] = jnp.broadcast_to(
        jnp.sum(jnp.where(spots, probe, 0.0), axis=0, keepdims=True), probe_ref.shape
    )
    vec_ref[...] = jnp.broadcast_to(vector, vec_ref.shape)
    lane = lax.broadcasted_iota(jnp.int32, scal_ref.shape, 1)
    scal_ref[...] = jnp.where(lane == 0, shrink, sine)
    y = place_ref[0]
    own_ref[...] = col_ref[pl.ds(pl.multiple_of(y * 8 * own, 8 * own), 8 * own), :]
    for c in range(2):
        for zl in range(4):
            some = pl.ds((c * 4 + zl) * own, own)
            rot_ref[some, :] = pairs_ref[zl * 8 + y * 2 + c, :, wide] + own_ref[some, :] * tail


def finish(place, pairs, tangent, basis, inputs):
    rank = basis.shape[1]
    vmem = pl.BlockSpec(memory_space=pltpu.VMEM)
    return pl.pallas_call(
        finish_kernel,
        out_shape=(
            jax.ShapeDtypeStruct((8, rank), F32),
            jax.ShapeDtypeStruct((rank // 4, 1), F32),
            jax.ShapeDtypeStruct((rank // 4, rank), F32),
            jax.ShapeDtypeStruct((tangent.shape[0], 1), F32),
            jax.ShapeDtypeStruct((8, inputs.shape[0]), F32),
            jax.ShapeDtypeStruct((8, 128), F32),
        ),
        in_specs=[pl.BlockSpec(memory_space=pltpu.SMEM)] + [vmem] * 4,
        out_specs=(vmem,) * 6,
        scratch_shapes=[pltpu.VMEM((rank, rank), F32)] * 2 + [pltpu.VMEM((rank, 1), F32)],
        compiler_params=pltpu.CompilerParams(vmem_limit_bytes=40 * 1024 * 1024),
    )(place, pairs, tangent, basis, inputs)


def turn_kernel(rot_ref, moments_ref, out_ref):
    for which in range(2):
        rows = jnp.concatenate(
            [
                moments_ref[y, c, zl, which]
                for zl in range(4)
                for y in range(4)
                for c in range(2)
            ],
            axis=0,
        )
        rot = rot_ref[...]
        out_ref[which] = exact(rot if which == 0 else rot * rot, rows, NN)


def turn(rot, moments):
    cols = moments.shape[-1]
    vmem = pl.BlockSpec(memory_space=pltpu.VMEM)
    return pl.pallas_call(
        turn_kernel,
        out_shape=jax.ShapeDtypeStruct((2, rot.shape[0], cols), F32),
        in_specs=[vmem] * 2,
        out_specs=vmem,
        compiler_params=pltpu.CompilerParams(vmem_limit_bytes=24 * 1024 * 1024),
    )(rot, moments)


def back_kernel(place_ref, grads_ref, mine_ref, other_ref, out_ref):
    rows, cols = mine_ref.shape[2:]
    for half, low_ref in enumerate((mine_ref, other_ref)):
        c = place_ref[2] if half == 0 else 1 - place_ref[2]
        wide = grads_ref[:, pl.ds(pl.multiple_of(c * 4 * cols, 128), 4 * cols)]
        for zl in range(4):
            block = wide[:, zl * cols : (zl + 1) * cols]
            for y in range(4):
                part = low(block, low_ref[y, zl], NT)
                if half + zl > 0:
                    part += out_ref[:, y * rows : (y + 1) * rows]
                out_ref[:, y * rows : (y + 1) * rows] = part


def back_product(place, grads, mine, other):
    tokens = grads.shape[0]
    vmem = pl.BlockSpec(memory_space=pltpu.VMEM)
    return pl.pallas_call(
        back_kernel,
        out_shape=jax.ShapeDtypeStruct((tokens, 4 * mine.shape[2]), F32),
        in_specs=[pl.BlockSpec(memory_space=pltpu.SMEM)] + [vmem] * 3,
        out_specs=vmem,
        compiler_params=pltpu.CompilerParams(vmem_limit_bytes=24 * 1024 * 1024),
    )(place, grads, mine, other)


def pair_kernel(place_ref, mine_ref, other_ref, basis_ref, tangent_ref, out_ref, total_ref):
    half, rank = mine_ref.shape
    own = out_ref.shape[0]
    c = place_ref[2]
    tangent_ref[pl.ds(pl.multiple_of(c * half, half), half), :] = mine_ref[...]
    tangent_ref[pl.ds(pl.multiple_of((1 - c) * half, half), half), :] = other_ref[...]
    start = pl.multiple_of((place_ref[1] // 8) * 128, 128)
    spot = pl.multiple_of((place_ref[1] % 8) * own, own)
    total_ref[...] = jnp.zeros_like(total_ref)

    def step(k, carry):
        some = pl.ds(pl.multiple_of(k * 256, 256), 256)
        tan = tangent_ref[some, pl.ds(start, 128)]
        bas = basis_ref[some, pl.ds(start, 128)]
        total_ref[:, pl.ds(0, rank)] += exact(tan, tangent_ref[some, :], TN)
        total_ref[:, pl.ds(rank, rank)] += exact(tan, basis_ref[some, :], TN)
        total_ref[:, pl.ds(2 * rank, rank)] += exact(bas, basis_ref[some, :], TN)
        return carry

    lax.fori_loop(0, 2 * half // 256, step, 0)
    out_ref[...] = total_ref[pl.ds(spot, own), :]


def pair_products(place, mine, other, basis):
    rank = basis.shape[1]
    vmem = pl.BlockSpec(memory_space=pltpu.VMEM)
    return pl.pallas_call(
        pair_kernel,
        out_shape=(
            jax.ShapeDtypeStruct(basis.shape, F32),
            jax.ShapeDtypeStruct((rank // 32, 3 * rank), F32),
        ),
        in_specs=[pl.BlockSpec(memory_space=pltpu.SMEM)] + [vmem] * 3,
        out_specs=(vmem,) * 2,
        scratch_shapes=[pltpu.VMEM((128, 3 * rank), F32)],
        compiler_params=pltpu.CompilerParams(vmem_limit_bytes=24 * 1024 * 1024),
    )(place, mine, other, basis)


CZ = ("c", "zl")


def body(layer_inputs, out_grads, basis, first, second):
    tokens, feats = layer_inputs.shape
    cols = out_grads.shape[1] // 8
    rank = basis.shape[1]
    own = rank // 32
    zl, y, c = (lax.axis_index(a) for a in DP)
    piece = (c * 4 + y) * 4 + zl
    part = feats // 32
    place = jnp.stack([y, piece, c]).astype(jnp.int32)

    def to_inner(value):
        lead = value.shape[:-1]
        k = len(lead)
        split = value.reshape(*lead, 4, 4, 2, own)
        return split.transpose(*range(k), k + 1, k + 2, k, k + 3).reshape(*lead, rank)

    grads = out_grads.reshape(tokens, 8, cols).transpose(1, 0, 2)
    inputs = layer_inputs.reshape(tokens, 2, 4, 4, part).transpose(1, 3, 0, 2, 4)
    both = jnp.concatenate([inputs.reshape(8, tokens, 4 * part), grads], axis=2)
    both = lax.all_to_all(both, CZ, 0, 0, tiled=True)
    inputs_all = both[:, :, : 4 * part]
    grads_all = both[:, :, 4 * part :]
    moments = jnp.stack([first, second]).reshape(2, own, 8, cols).transpose(2, 0, 1, 3)
    moments = lax.all_to_all(moments, CZ, 0, 0, tiled=True)
    moments = stack(moments, "y", True).reshape(4, 2, 4, 2, own, cols)

    basis_low = basis.astype(BF16)
    score_part = jnp.dot(layer_inputs, basis_low, preferred_element_type=F32)
    score_own = scatter_near(score_part, "x")
    score_own = all_sum(score_own, "zh")
    scores = stack(to_inner(score_own.astype(BF16)), "x").reshape(tokens, rank)
    scores_all = stack(stack(scores, "zl"), "c").reshape(8 * tokens, rank)

    grad_part = low(scores_all, grads_all.reshape(8 * tokens, cols), TN)
    grad_own = scatter_sum(grad_part, "y")
    grad_low = stack_yz(grad_own.astype(BF16))
    grad_far = shift(grad_low, "c", 1)
    back_part = back_product(place, out_grads, grad_low, grad_far)
    back_own = scatter_sum(back_part, "x")
    back_own = all_sum(back_own, "zh")
    backward = stack(back_own.astype(BF16), "x", True).reshape(tokens, rank)
    backward_all = stack(stack(backward, "zl", True), "c").reshape(8 * tokens, rank)
    tangent_part = low(inputs_all.reshape(8 * tokens, 4 * part), backward_all, TN)
    tan_near = stack_yz(scatter_sum(tangent_part, "y"), True).reshape(feats // 2, rank)
    tan_far = shift(tan_near, "c", 1)

    tangent, pair = pair_products(place, tan_near, tan_far, basis)
    pair = stack(all_sum(pair, "zh"), "x", True).sum(0)
    pairs = stack(stack_yz(pair, True), "c").reshape(32, own, 3 * rank)
    vec, vec_own, rot_own, step, probe_part, scal = finish(
        place, pairs, tangent, basis, layer_inputs
    )
    new_basis = basis + step * vec[:1]
    probe = all_sum(probe_part, "zh")
    probe = stack(probe, "x", True).sum(0)[0].astype(BF16)
    along_part = jnp.dot(probe, out_grads, preferred_element_type=F32).reshape(2, 4, cols)
    lead_part = jnp.sum(vec_own * grad_own, axis=0)
    mine = (jnp.arange(2)[:, None] == c) & (jnp.arange(4)[None] == zl)
    push_part = scal[0, 1] * along_part + jnp.where(mine[:, :, None], scal[0, 0] * lead_part, 0.0)
    push_many = jnp.broadcast_to(push_part.transpose(1, 0, 2)[:, None], (4, 4, 2, cols))
    push = lax.all_to_all(push_many.reshape(32, cols), DP, 0, 0, tiled=True).sum(0)

    turned = turn(rot_own, moments)
    grad_new = grad_own + vec_own * push
    moved = jnp.stack(
        [0.9 * turned[0] + 0.1 * grad_new, 0.95 * turned[1] + 0.05 * grad_new * grad_new]
    )
    moved = moved.reshape(2, 8, own, cols).transpose(1, 0, 2, 3)
    moved = lax.all_to_all(moved, CZ, 0, 0, tiled=True)
    moved = moved.transpose(1, 2, 0, 3).reshape(2, own, 8 * cols)
    new_first, new_second = moved[0], moved[1]
    update = new_first / (jnp.sqrt(new_second) + 1e-06)
    return (new_basis, new_first, new_second, update)


def solution(mesh):
    fine = Mesh(mesh.devices.reshape(4, 4, 2, 2, 4), DP + TE)
    return jax.shard_map(
        body,
        mesh=fine,
        in_specs=(P(DP, TE), P(DP, TE), P(TE, None), P(DP, TE), P(DP, TE)),
        out_specs=(P(TE, None), P(DP, TE), P(DP, TE), P(DP, TE)),
        check_vma=False,
    )
```

```python
import jax
import jax.numpy as jnp
from jax import lax
from jax.experimental import pallas as pl
from jax.experimental.pallas import tpu as pltpu
from jax.sharding import Mesh, PartitionSpec as P

PI_STEPS = 6
EXACT = lax.Precision.HIGHEST
F32 = jnp.float32
BF16 = jnp.bfloat16
SIZES = {"zl": 4, "y": 4, "c": 2, "zh": 2, "x": 4}
DP = ("zl", "y", "c")
TE = ("zh", "x")


def shift(value, axis, k):
    n = SIZES[axis]
    return lax.ppermute(value, axis, [(i, (i - k) % n) for i in range(n)])


def all_sum(value, axis):
    if SIZES[axis] == 2:
        return value + shift(value, axis, 1)
    one, two, three = (shift(value, axis, k) for k in (1, 2, 3))
    return (value + two) + (one + three)


def scatter_sum(value, axis):
    n = SIZES[axis]
    moved = lax.all_to_all(value, axis, 0, 0, tiled=True)
    return moved.reshape(n, value.shape[0] // n, *value.shape[1:]).sum(0)


def scatter_near(value, axis):
    n = SIZES[axis]
    me = lax.axis_index(axis)
    rows = value.shape[0] // n

    def mine(k):
        return lax.dynamic_slice_in_dim(value, ((me + k) % n) * rows, rows, 0)

    one, two, three = (
        lax.ppermute(mine(k), axis, [(i, (i + k) % n) for i in range(n)]) for k in (1, 2, 3)
    )
    return (mine(0) + two) + (one + three)


def stack(value, axis, at_once=False):
    n = SIZES[axis]
    if at_once:
        many = jnp.broadcast_to(value[None], (n, *value.shape))
        return lax.all_to_all(many, axis, 0, 0, tiled=True)
    me = lax.axis_index(axis)
    if n == 2:
        other = shift(value, axis, 1)
        return jnp.where(me == 0, jnp.stack([value, other]), jnp.stack([other, value]))
    out = jnp.zeros((n, *value.shape), value.dtype)
    out = lax.dynamic_update_slice_in_dim(out, value[None], me, 0)
    for k in range(1, n):
        out = lax.dynamic_update_slice_in_dim(out, shift(value, axis, k)[None], (me + k) % n, 0)
    return out


def rows_of_x(value):
    near = [value] + [shift(value, "x", k) for k in (1, 2, 3)]
    twice = jnp.concatenate(near + near, axis=0)
    rows = value.shape[0]
    return lax.dynamic_slice_in_dim(twice, ((4 - lax.axis_index("x")) % 4) * rows, 4 * rows, 0)


def stack_yz(value, at_once=False):
    value = stack(value, "zl")
    return stack(value, "y", at_once)


NN, NT, TN = ((1,), (0,)), ((1,), (1,)), ((0,), (0,))


def exact(left, right, dims):
    return lax.dot_general(left, right, (dims, ((), ())), precision=EXACT, preferred_element_type=F32)


def low(left, right, dims):
    return lax.dot_general(left, right, (dims, ((), ())), preferred_element_type=F32)


def finish_kernel(
    place_ref, pairs_ref, tangent_ref, basis_ref, inputs_ref,
    vec_ref, own_ref, rot_ref, step_ref, probe_ref, scal_ref,
    kernel_ref, mixed_ref, col_ref,
):
    rank = kernel_ref.shape[0]
    own = rank // 32
    coup = pl.ds(rank, rank)
    wide = pl.ds(2 * rank, rank)

    half = rank // 2
    mixed_ref[...] = 2.0 * pairs_ref[:, :, coup].reshape(rank, rank)
    kernel_ref[...] = pairs_ref[:, :, pl.ds(0, rank)].reshape(rank, rank)

    def mix(i, carry):
        k, n = i // 2, i % 2
        out = pl.ds(pl.multiple_of(n * half, half), half)
        mixed_ref[:, out] -= exact(
            pairs_ref[:, :, pl.ds(pl.multiple_of(rank + k * half, half), half)].reshape(rank, half),
            pairs_ref[
                pl.ds(k * 16, 16), :, pl.ds(pl.multiple_of(2 * rank + n * half, half), half)
            ].reshape(half, half),
            NN,
        )
        return carry

    def fill(i, carry):
        k, n = i // 2, i % 2
        out = pl.ds(pl.multiple_of(n * half, half), half)
        kernel_ref[:, out] -= exact(
            mixed_ref[:, pl.ds(pl.multiple_of(k * half, half), half)],
            pairs_ref[
                pl.ds(n * 16, 16), :, pl.ds(pl.multiple_of(rank + k * half, half), half)
            ].reshape(half, half),
            NT,
        )
        return carry

    lax.fori_loop(0, 4, mix, 0)
    lax.fori_loop(0, 4, fill, 0)
    rows = lax.broadcasted_iota(jnp.int32, (rank, rank), 0)
    lanes = lax.broadcasted_iota(jnp.int32, (rank, rank), 1)
    total = jnp.sum(jnp.where(rows == lanes, kernel_ref[...], 0.0), keepdims=True)
    inv = 1.0 / total

    def to_row(col):
        return jnp.sum(kernel_ref[...] * col, axis=0, keepdims=True) * inv

    def to_col(row):
        return jnp.sum(kernel_ref[...] * row, axis=1, keepdims=True) * inv

    def unit(vec):
        return vec / jnp.sqrt(jnp.sum(vec * vec, keepdims=True) + 1e-12)

    col_ref[...] = jnp.full((rank, 1), 1.0, F32) / jnp.sqrt(F32(rank))

    def sweep(i, carry):
        col_ref[...] = unit(to_col(unit(to_row(col_ref[...]))))
        return carry

    lax.fori_loop(0, PI_STEPS // 2, sweep, 0)
    col = col_ref[...]
    last = to_row(col)
    row = jnp.sum(jnp.where(rows == lanes, col, 0.0), axis=0, keepdims=True)
    ratio = jnp.sum(row * last, keepdims=True)
    group = lanes // own
    source = ((group // 2) % 4) * 8 + (group % 2) * 4 + group // 8
    vector = jnp.sum(jnp.where(rows == source * own + lanes % own, col, 0.0), axis=0, keepdims=True)
    theta = 4.0 * jnp.sqrt(ratio)
    sigma = jnp.sqrt(total * ratio + 1e-06)
    shrink = jnp.cos(theta) - 1.0
    sine = jnp.sin(theta)

    coup_row = jnp.sum(pairs_ref[:, :, coup].reshape(rank, rank) * col, axis=0, keepdims=True)
    gram = pairs_ref[:, :, wide].reshape(rank, rank)

    def flip(vec):
        return jnp.sum(jnp.where(rows == lanes, vec, 0.0), axis=1, keepdims=True)

    tail = shrink * jnp.sum(gram * flip(vector), axis=0, keepdims=True) + (sine / sigma) * (
        coup_row - jnp.sum(gram * flip(coup_row), axis=0, keepdims=True)
    )
    size = inputs_ref.shape[0]
    feats = basis_ref.shape[0]

    def rise(i, carry):
        some = pl.ds(pl.multiple_of(i * size, size), size)
        old = basis_ref[some, :]
        left = jnp.sum(tangent_ref[some, :] * row - old * coup_row, axis=1, keepdims=True) / sigma
        step_ref[some, :] = shrink * jnp.sum(old * vector, axis=1, keepdims=True) + sine * left
        wide_left = jnp.broadcast_to(left, (size, size)).astype(BF16)
        return carry + low(inputs_ref[:, some], wide_left, NN)

    probe = lax.fori_loop(0, feats // size, rise, jnp.zeros((size, size), F32))
    spots = lax.broadcasted_iota(jnp.int32, (size, size), 0) == lax.broadcasted_iota(
        jnp.int32, (size, size), 1
    )
    probe_ref[...] = jnp.broadcast_to(
        jnp.sum(jnp.where(spots, probe, 0.0), axis=0, keepdims=True), probe_ref.shape
    )
    vec_ref[...] = jnp.broadcast_to(vector, vec_ref.shape)
    lane = lax.broadcasted_iota(jnp.int32, scal_ref.shape, 1)
    scal_ref[...] = jnp.where(lane == 0, shrink, sine)
    y = place_ref[0]
    own_ref[...] = col_ref[pl.ds(pl.multiple_of(y * 8 * own, 8 * own), 8 * own), :]
    for c in range(2):
        for zl in range(4):
            some = pl.ds((c * 4 + zl) * own, own)
            rot_ref[some, :] = pairs_ref[zl * 8 + y * 2 + c, :, wide] + own_ref[some, :] * tail


def finish(place, pairs, tangent, basis, inputs):
    rank = basis.shape[1]
    vmem = pl.BlockSpec(memory_space=pltpu.VMEM)
    return pl.pallas_call(
        finish_kernel,
        out_shape=(
            jax.ShapeDtypeStruct((8, rank), F32),
            jax.ShapeDtypeStruct((rank // 4, 1), F32),
            jax.ShapeDtypeStruct((rank // 4, rank), F32),
            jax.ShapeDtypeStruct((tangent.shape[0], 1), F32),
            jax.ShapeDtypeStruct((8, inputs.shape[0]), F32),
            jax.ShapeDtypeStruct((8, 128), F32),
        ),
        in_specs=[pl.BlockSpec(memory_space=pltpu.SMEM)] + [vmem] * 4,
        out_specs=(vmem,) * 6,
        scratch_shapes=[pltpu.VMEM((rank, rank), F32)] * 2 + [pltpu.VMEM((rank, 1), F32)],
        compiler_params=pltpu.CompilerParams(vmem_limit_bytes=40 * 1024 * 1024),
    )(place, pairs, tangent, basis, inputs)


def turn_kernel(rot_ref, moments_ref, out_ref):
    for which in range(2):
        rows = jnp.concatenate(
            [
                moments_ref[y, c, zl, which]
                for zl in range(4)
                for y in range(4)
                for c in range(2)
            ],
            axis=0,
        )
        rot = rot_ref[...]
        out_ref[which] = exact(rot if which == 0 else rot * rot, rows, NN)


def turn(rot, moments):
    cols = moments.shape[-1]
    vmem = pl.BlockSpec(memory_space=pltpu.VMEM)
    return pl.pallas_call(
        turn_kernel,
        out_shape=jax.ShapeDtypeStruct((2, rot.shape[0], cols), F32),
        in_specs=[vmem] * 2,
        out_specs=vmem,
        compiler_params=pltpu.CompilerParams(vmem_limit_bytes=24 * 1024 * 1024),
    )(rot, moments)


def back_kernel(place_ref, grads_ref, mine_ref, other_ref, out_ref):
    rows, cols = mine_ref.shape[2:]
    for half, low_ref in enumerate((mine_ref, other_ref)):
        c = place_ref[2] if half == 0 else 1 - place_ref[2]
        wide = grads_ref[:, pl.ds(pl.multiple_of(c * 4 * cols, 128), 4 * cols)]
        for zl in range(4):
            block = wide[:, zl * cols : (zl + 1) * cols]
            for y in range(4):
                part = low(block, low_ref[y, zl], NT)
                if half + zl > 0:
                    part += out_ref[:, y * rows : (y + 1) * rows]
                out_ref[:, y * rows : (y + 1) * rows] = part


def back_product(place, grads, mine, other):
    tokens = grads.shape[0]
    vmem = pl.BlockSpec(memory_space=pltpu.VMEM)
    return pl.pallas_call(
        back_kernel,
        out_shape=jax.ShapeDtypeStruct((tokens, 4 * mine.shape[2]), F32),
        in_specs=[pl.BlockSpec(memory_space=pltpu.SMEM)] + [vmem] * 3,
        out_specs=vmem,
        compiler_params=pltpu.CompilerParams(vmem_limit_bytes=24 * 1024 * 1024),
    )(place, grads, mine, other)


def pair_kernel(place_ref, mine_ref, other_ref, basis_ref, tangent_ref, out_ref, total_ref):
    half, rank = mine_ref.shape
    own = out_ref.shape[0]
    c = place_ref[2]
    tangent_ref[pl.ds(pl.multiple_of(c * half, half), half), :] = mine_ref[...]
    tangent_ref[pl.ds(pl.multiple_of((1 - c) * half, half), half), :] = other_ref[...]
    start = pl.multiple_of((place_ref[1] // 8) * 128, 128)
    spot = pl.multiple_of((place_ref[1] % 8) * own, own)
    total_ref[...] = jnp.zeros_like(total_ref)

    def step(k, carry):
        some = pl.ds(pl.multiple_of(k * 256, 256), 256)
        tan = tangent_ref[some, pl.ds(start, 128)]
        bas = basis_ref[some, pl.ds(start, 128)]
        total_ref[:, pl.ds(0, rank)] += exact(tan, tangent_ref[some, :], TN)
        total_ref[:, pl.ds(rank, rank)] += exact(tan, basis_ref[some, :], TN)
        total_ref[:, pl.ds(2 * rank, rank)] += exact(bas, basis_ref[some, :], TN)
        return carry

    lax.fori_loop(0, 2 * half // 256, step, 0)
    out_ref[...] = total_ref[pl.ds(spot, own), :]


def pair_products(place, mine, other, basis):
    rank = basis.shape[1]
    vmem = pl.BlockSpec(memory_space=pltpu.VMEM)
    return pl.pallas_call(
        pair_kernel,
        out_shape=(
            jax.ShapeDtypeStruct(basis.shape, F32),
            jax.ShapeDtypeStruct((rank // 32, 3 * rank), F32),
        ),
        in_specs=[pl.BlockSpec(memory_space=pltpu.SMEM)] + [vmem] * 3,
        out_specs=(vmem,) * 2,
        scratch_shapes=[pltpu.VMEM((128, 3 * rank), F32)],
        compiler_params=pltpu.CompilerParams(vmem_limit_bytes=24 * 1024 * 1024),
    )(place, mine, other, basis)


CZ = ("c", "zl")


def body(layer_inputs, out_grads, basis, first, second):
    tokens, feats = layer_inputs.shape
    cols = out_grads.shape[1] // 8
    rank = basis.shape[1]
    own = rank // 32
    zl, y, c = (lax.axis_index(a) for a in DP)
    piece = (c * 4 + y) * 4 + zl
    part = feats // 32
    place = jnp.stack([y, piece, c]).astype(jnp.int32)

    def to_inner(value):
        lead = value.shape[:-1]
        k = len(lead)
        split = value.reshape(*lead, 4, 4, 2, own)
        return split.transpose(*range(k), k + 1, k + 2, k, k + 3).reshape(*lead, rank)

    grads = out_grads.reshape(tokens, 8, cols).transpose(1, 0, 2)
    grads_all = lax.all_to_all(grads, CZ, 0, 0, tiled=True)
    inputs = layer_inputs.reshape(tokens, 2, 4, 4, part).transpose(1, 3, 0, 2, 4)
    inputs_all = lax.all_to_all(inputs.reshape(8, tokens, 4 * part), CZ, 0, 0, tiled=True)
    moments = jnp.stack([first, second]).reshape(2, own, 8, cols).transpose(2, 0, 1, 3)
    moments = lax.all_to_all(moments, CZ, 0, 0, tiled=True)
    moments = stack(moments, "y", True).reshape(4, 2, 4, 2, own, cols)

    basis_low = basis.astype(BF16)
    score_part = jnp.dot(layer_inputs, basis_low, preferred_element_type=F32)
    score_own = scatter_near(score_part, "x")
    score_own = all_sum(score_own, "zh")
    scores = rows_of_x(to_inner(score_own.astype(BF16)))
    scores_all = stack(stack(scores, "zl"), "c").reshape(8 * tokens, rank)

    grad_part = low(scores_all, grads_all.reshape(8 * tokens, cols), TN)
    grad_own = scatter_sum(grad_part, "y")
    grad_low = stack_yz(grad_own.astype(BF16))
    grad_far = shift(grad_low, "c", 1)
    back_part = back_product(place, out_grads, grad_low, grad_far)
    back_own = scatter_near(back_part, "x")
    back_own = all_sum(back_own, "zh")
    backward = rows_of_x(back_own.astype(BF16))
    backward_all = stack(stack(backward, "zl"), "c").reshape(8 * tokens, rank)
    tangent_part = low(inputs_all.reshape(8 * tokens, 4 * part), backward_all, TN)
    tan_near = stack_yz(scatter_sum(tangent_part, "y"), True).reshape(feats // 2, rank)
    tan_far = shift(tan_near, "c", 1)

    tangent, pair = pair_products(place, tan_near, tan_far, basis)
    pair = all_sum(pair, "zh")
    pair = all_sum(pair, "x")
    pairs = stack(stack_yz(pair, True), "c").reshape(32, own, 3 * rank)
    vec, vec_own, rot_own, step, probe_part, scal = finish(
        place, pairs, tangent, basis, layer_inputs
    )
    new_basis = basis + step * vec[:1]
    probe = stack(all_sum(probe_part, "zh"), "x", True).sum(0)[0].astype(BF16)
    along_part = jnp.dot(probe, out_grads, preferred_element_type=F32).reshape(2, 4, cols)
    lead_part = jnp.sum(vec_own * grad_own, axis=0)
    mine = (jnp.arange(2)[:, None] == c) & (jnp.arange(4)[None] == zl)
    push_part = scal[0, 1] * along_part + jnp.where(mine[:, :, None], scal[0, 0] * lead_part, 0.0)
    push_many = jnp.broadcast_to(push_part.transpose(1, 0, 2)[:, None], (4, 4, 2, cols))
    push = lax.all_to_all(push_many.reshape(32, cols), DP, 0, 0, tiled=True).sum(0)

    turned = turn(rot_own, moments)
    grad_new = grad_own + vec_own * push
    moved = jnp.stack(
        [0.9 * turned[0] + 0.1 * grad_new, 0.95 * turned[1] + 0.05 * grad_new * grad_new]
    )
    moved = moved.reshape(2, 8, own, cols).transpose(1, 0, 2, 3)
    moved = lax.all_to_all(moved, CZ, 0, 0, tiled=True)
    moved = moved.transpose(1, 2, 0, 3).reshape(2, own, 8 * cols)
    new_first, new_second = moved[0], moved[1]
    update = new_first / (jnp.sqrt(new_second) + 1e-06)
    return (new_basis, new_first, new_second, update)


def solution(mesh):
    fine = Mesh(mesh.devices.reshape(4, 4, 2, 2, 4), DP + TE)
    return jax.shard_map(
        body,
        mesh=fine,
        in_specs=(P(DP, TE), P(DP, TE), P(TE, None), P(DP, TE), P(DP, TE)),
        out_specs=(P(TE, None), P(DP, TE), P(DP, TE), P(DP, TE)),
        check_vma=False,
    )
```

```python
import jax
import jax.numpy as jnp
from jax import lax
from jax.experimental import pallas as pl
from jax.experimental.pallas import tpu as pltpu
from jax.sharding import Mesh, PartitionSpec as P

PI_STEPS = 6
EXACT = lax.Precision.HIGHEST
F32 = jnp.float32
BF16 = jnp.bfloat16
SIZES = {"zl": 4, "y": 4, "c": 2, "zh": 2, "x": 4}
DP = ("zl", "y", "c")
TE = ("zh", "x")


def shift(value, axis, k):
    n = SIZES[axis]
    return lax.ppermute(value, axis, [(i, (i - k) % n) for i in range(n)])


def all_sum(value, axis):
    if SIZES[axis] == 2:
        return value + shift(value, axis, 1)
    one, two, three = (shift(value, axis, k) for k in (1, 2, 3))
    return (value + two) + (one + three)


def scatter_sum(value, axis):
    n = SIZES[axis]
    moved = lax.all_to_all(value, axis, 0, 0, tiled=True)
    return moved.reshape(n, value.shape[0] // n, *value.shape[1:]).sum(0)


def scatter_near(value, axis):
    n = SIZES[axis]
    me = lax.axis_index(axis)
    rows = value.shape[0] // n

    def mine(k):
        return lax.dynamic_slice_in_dim(value, ((me + k) % n) * rows, rows, 0)

    one, two, three = (
        lax.ppermute(mine(k), axis, [(i, (i + k) % n) for i in range(n)]) for k in (1, 2, 3)
    )
    return (mine(0) + two) + (one + three)


def stack(value, axis, at_once=False):
    n = SIZES[axis]
    if at_once:
        many = jnp.broadcast_to(value[None], (n, *value.shape))
        return lax.all_to_all(many, axis, 0, 0, tiled=True)
    me = lax.axis_index(axis)
    if n == 2:
        other = shift(value, axis, 1)
        return jnp.where(me == 0, jnp.stack([value, other]), jnp.stack([other, value]))
    out = jnp.zeros((n, *value.shape), value.dtype)
    out = lax.dynamic_update_slice_in_dim(out, value[None], me, 0)
    for k in range(1, n):
        out = lax.dynamic_update_slice_in_dim(out, shift(value, axis, k)[None], (me + k) % n, 0)
    return out


def rows_of_x(value):
    near = [value] + [shift(value, "x", k) for k in (1, 2, 3)]
    twice = jnp.concatenate(near + near, axis=0)
    rows = value.shape[0]
    return lax.dynamic_slice_in_dim(twice, ((4 - lax.axis_index("x")) % 4) * rows, 4 * rows, 0)


def stack_yz(value, at_once=False):
    value = stack(value, "zl")
    return stack(value, "y", at_once)


NN, NT, TN = ((1,), (0,)), ((1,), (1,)), ((0,), (0,))


def exact(left, right, dims):
    return lax.dot_general(left, right, (dims, ((), ())), precision=EXACT, preferred_element_type=F32)


def low(left, right, dims):
    return lax.dot_general(left, right, (dims, ((), ())), preferred_element_type=F32)


def finish_kernel(
    place_ref, pairs_ref, tangent_ref, basis_ref, inputs_ref,
    vec_ref, own_ref, rot_ref, step_ref, probe_ref, scal_ref,
    kernel_ref, mixed_ref, gram_ref, col_ref,
):
    rank = kernel_ref.shape[0]
    own = rank // 32
    quarter = rank // 4
    first = 3 * quarter
    coup = pl.ds(first, rank)
    for full_ref, start in ((kernel_ref, 0), (gram_ref, first + rank)):
        for q in range(4):
            for k in range(3):
                block = pairs_ref[
                    q * 8 : (q + 1) * 8, :, start + k * quarter : start + (k + 1) * quarter
                ].reshape(quarter, quarter)
                r = (q + k) % 4
                full_ref[q * quarter : (q + 1) * quarter, r * quarter : (r + 1) * quarter] = block
                if k == 1:
                    full_ref[r * quarter : (r + 1) * quarter, q * quarter : (q + 1) * quarter] = block.T

    half = rank // 2
    mixed_ref[...] = 2.0 * pairs_ref[:, :, coup].reshape(rank, rank)

    def mix(i, carry):
        k, n = i // 2, i % 2
        out = pl.ds(pl.multiple_of(n * half, half), half)
        mixed_ref[:, out] -= exact(
            pairs_ref[:, :, pl.ds(pl.multiple_of(first + k * half, quarter), half)].reshape(rank, half),
            gram_ref[pl.ds(pl.multiple_of(k * half, half), half), out],
            NN,
        )
        return carry

    def fill(i, carry):
        k, n = i // 2, i % 2
        out = pl.ds(pl.multiple_of(n * half, half), half)
        kernel_ref[:, out] -= exact(
            mixed_ref[:, pl.ds(pl.multiple_of(k * half, half), half)],
            pairs_ref[
                pl.ds(n * 16, 16), :, pl.ds(pl.multiple_of(first + k * half, quarter), half)
            ].reshape(half, half),
            NT,
        )
        return carry

    lax.fori_loop(0, 4, mix, 0)
    lax.fori_loop(0, 4, fill, 0)
    rows = lax.broadcasted_iota(jnp.int32, (rank, rank), 0)
    lanes = lax.broadcasted_iota(jnp.int32, (rank, rank), 1)
    total = jnp.sum(jnp.where(rows == lanes, kernel_ref[...], 0.0), keepdims=True)
    inv = 1.0 / total

    def to_row(col):
        return jnp.sum(kernel_ref[...] * col, axis=0, keepdims=True) * inv

    def to_col(row):
        return jnp.sum(kernel_ref[...] * row, axis=1, keepdims=True) * inv

    def unit(vec):
        return vec / jnp.sqrt(jnp.sum(vec * vec, keepdims=True) + 1e-12)

    col_ref[...] = jnp.full((rank, 1), 1.0, F32) / jnp.sqrt(F32(rank))

    def sweep(i, carry):
        col_ref[...] = unit(to_col(unit(to_row(col_ref[...]))))
        return carry

    lax.fori_loop(0, PI_STEPS // 2, sweep, 0)
    col = col_ref[...]
    last = to_row(col)
    row = jnp.sum(jnp.where(rows == lanes, col, 0.0), axis=0, keepdims=True)
    ratio = jnp.sum(row * last, keepdims=True)
    group = lanes // own
    source = ((group // 2) % 4) * 8 + (group % 2) * 4 + group // 8
    vector = jnp.sum(jnp.where(rows == source * own + lanes % own, col, 0.0), axis=0, keepdims=True)
    theta = 4.0 * jnp.sqrt(ratio)
    sigma = jnp.sqrt(total * ratio + 1e-06)
    shrink = jnp.cos(theta) - 1.0
    sine = jnp.sin(theta)

    coup_row = jnp.sum(pairs_ref[:, :, coup].reshape(rank, rank) * col, axis=0, keepdims=True)
    gram = gram_ref[...]

    def flip(vec):
        return jnp.sum(jnp.where(rows == lanes, vec, 0.0), axis=1, keepdims=True)

    tail = shrink * jnp.sum(gram * flip(vector), axis=0, keepdims=True) + (sine / sigma) * (
        coup_row - jnp.sum(gram * flip(coup_row), axis=0, keepdims=True)
    )
    size = inputs_ref.shape[0]
    feats = basis_ref.shape[0]

    def rise(i, carry):
        some = pl.ds(pl.multiple_of(i * size, size), size)
        old = basis_ref[some, :]
        left = jnp.sum(tangent_ref[some, :] * row - old * coup_row, axis=1, keepdims=True) / sigma
        step_ref[some, :] = shrink * jnp.sum(old * vector, axis=1, keepdims=True) + sine * left
        wide_left = jnp.broadcast_to(left, (size, size)).astype(BF16)
        return carry + low(inputs_ref[:, some], wide_left, NN)

    probe = lax.fori_loop(0, feats // size, rise, jnp.zeros((size, size), F32))
    spots = lax.broadcasted_iota(jnp.int32, (size, size), 0) == lax.broadcasted_iota(
        jnp.int32, (size, size), 1
    )
    probe_ref[...] = jnp.broadcast_to(
        jnp.sum(jnp.where(spots, probe, 0.0), axis=0, keepdims=True), probe_ref.shape
    )
    vec_ref[...] = jnp.broadcast_to(vector, vec_ref.shape)
    lane = lax.broadcasted_iota(jnp.int32, scal_ref.shape, 1)
    scal_ref[...] = jnp.where(lane == 0, shrink, sine)
    y = place_ref[0]
    own_ref[...] = col_ref[pl.ds(pl.multiple_of(y * 8 * own, 8 * own), 8 * own), :]
    for c in range(2):
        for zl in range(4):
            some = pl.ds((c * 4 + zl) * own, own)
            at = pl.ds(pl.multiple_of((zl * 8 + y * 2 + c) * own, own), own)
            rot_ref[some, :] = gram_ref[at, :] + own_ref[some, :] * tail


def finish(place, pairs, tangent, basis, inputs):
    rank = basis.shape[1]
    vmem = pl.BlockSpec(memory_space=pltpu.VMEM)
    return pl.pallas_call(
        finish_kernel,
        out_shape=(
            jax.ShapeDtypeStruct((8, rank), F32),
            jax.ShapeDtypeStruct((rank // 4, 1), F32),
            jax.ShapeDtypeStruct((rank // 4, rank), F32),
            jax.ShapeDtypeStruct((tangent.shape[0], 1), F32),
            jax.ShapeDtypeStruct((8, inputs.shape[0]), F32),
            jax.ShapeDtypeStruct((8, 128), F32),
        ),
        in_specs=[pl.BlockSpec(memory_space=pltpu.SMEM)] + [vmem] * 4,
        out_specs=(vmem,) * 6,
        scratch_shapes=[pltpu.VMEM((rank, rank), F32)] * 3 + [pltpu.VMEM((rank, 1), F32)],
        compiler_params=pltpu.CompilerParams(vmem_limit_bytes=40 * 1024 * 1024),
    )(place, pairs, tangent, basis, inputs)


def turn_kernel(rot_ref, moments_ref, out_ref):
    for which in range(2):
        rows = jnp.concatenate(
            [
                moments_ref[y, c, zl, which]
                for zl in range(4)
                for y in range(4)
                for c in range(2)
            ],
            axis=0,
        )
        rot = rot_ref[...]
        out_ref[which] = exact(rot if which == 0 else rot * rot, rows, NN)


def turn(rot, moments):
    cols = moments.shape[-1]
    vmem = pl.BlockSpec(memory_space=pltpu.VMEM)
    return pl.pallas_call(
        turn_kernel,
        out_shape=jax.ShapeDtypeStruct((2, rot.shape[0], cols), F32),
        in_specs=[vmem] * 2,
        out_specs=vmem,
        compiler_params=pltpu.CompilerParams(vmem_limit_bytes=24 * 1024 * 1024),
    )(rot, moments)


def back_kernel(place_ref, grads_ref, mine_ref, other_ref, out_ref):
    rows, cols = mine_ref.shape[2:]
    for half, low_ref in enumerate((mine_ref, other_ref)):
        c = place_ref[2] if half == 0 else 1 - place_ref[2]
        wide = grads_ref[:, pl.ds(pl.multiple_of(c * 4 * cols, 128), 4 * cols)]
        for zl in range(4):
            block = wide[:, zl * cols : (zl + 1) * cols]
            for y in range(4):
                part = low(block, low_ref[y, zl], NT)
                if half + zl > 0:
                    part += out_ref[:, y * rows : (y + 1) * rows]
                out_ref[:, y * rows : (y + 1) * rows] = part


def back_product(place, grads, mine, other):
    tokens = grads.shape[0]
    vmem = pl.BlockSpec(memory_space=pltpu.VMEM)
    return pl.pallas_call(
        back_kernel,
        out_shape=jax.ShapeDtypeStruct((tokens, 4 * mine.shape[2]), F32),
        in_specs=[pl.BlockSpec(memory_space=pltpu.SMEM)] + [vmem] * 3,
        out_specs=vmem,
        compiler_params=pltpu.CompilerParams(vmem_limit_bytes=24 * 1024 * 1024),
    )(place, grads, mine, other)


def pair_kernel(place_ref, mine_ref, other_ref, basis_ref, tangent_ref, out_ref, total_ref):
    half, rank = mine_ref.shape
    own = out_ref.shape[0]
    c = place_ref[2]
    tangent_ref[pl.ds(pl.multiple_of(c * half, half), half), :] = mine_ref[...]
    tangent_ref[pl.ds(pl.multiple_of((1 - c) * half, half), half), :] = other_ref[...]
    start = pl.multiple_of((place_ref[1] // 8) * 128, 128)
    spot = pl.multiple_of((place_ref[1] % 8) * own, own)
    total_ref[...] = jnp.zeros_like(total_ref)

    def step(k, carry):
        some = pl.ds(pl.multiple_of(k * 256, 256), 256)
        tan = tangent_ref[some, pl.ds(start, 128)]
        bas = basis_ref[some, pl.ds(start, 128)]
        total_ref[:, pl.ds(0, rank)] += exact(tan, tangent_ref[some, :], TN)
        total_ref[:, pl.ds(rank, rank)] += exact(tan, basis_ref[some, :], TN)
        total_ref[:, pl.ds(2 * rank, rank)] += exact(bas, basis_ref[some, :], TN)
        return carry

    lax.fori_loop(0, 2 * half // 256, step, 0)
    quarter = rank // 4
    some = pl.ds(spot, own)
    out_ref[:, 3 * quarter : 3 * quarter + rank] = total_ref[some, pl.ds(rank, rank)]
    for k in range(3):
        at = pl.multiple_of(((place_ref[1] // 8 + k) % 4) * quarter, quarter)
        out_ref[:, k * quarter : (k + 1) * quarter] = total_ref[some, pl.ds(at, quarter)]
        out_ref[:, 3 * quarter + rank + k * quarter : 3 * quarter + rank + (k + 1) * quarter] = (
            total_ref[some, pl.ds(2 * rank + at, quarter)]
        )


def pair_products(place, mine, other, basis):
    rank = basis.shape[1]
    vmem = pl.BlockSpec(memory_space=pltpu.VMEM)
    return pl.pallas_call(
        pair_kernel,
        out_shape=(
            jax.ShapeDtypeStruct(basis.shape, F32),
            jax.ShapeDtypeStruct((rank // 32, 5 * rank // 2), F32),
        ),
        in_specs=[pl.BlockSpec(memory_space=pltpu.SMEM)] + [vmem] * 3,
        out_specs=(vmem,) * 2,
        scratch_shapes=[pltpu.VMEM((128, 3 * rank), F32)],
        compiler_params=pltpu.CompilerParams(vmem_limit_bytes=24 * 1024 * 1024),
    )(place, mine, other, basis)


CZ = ("c", "zl")


def body(layer_inputs, out_grads, basis, first, second):
    tokens, feats = layer_inputs.shape
    cols = out_grads.shape[1] // 8
    rank = basis.shape[1]
    own = rank // 32
    zl, y, c = (lax.axis_index(a) for a in DP)
    piece = (c * 4 + y) * 4 + zl
    part = feats // 32
    place = jnp.stack([y, piece, c]).astype(jnp.int32)

    def to_inner(value):
        lead = value.shape[:-1]
        k = len(lead)
        split = value.reshape(*lead, 4, 4, 2, own)
        return split.transpose(*range(k), k + 1, k + 2, k, k + 3).reshape(*lead, rank)

    grads = out_grads.reshape(tokens, 8, cols).transpose(1, 0, 2)
    grads_all = lax.all_to_all(grads, CZ, 0, 0, tiled=True)
    inputs = layer_inputs.reshape(tokens, 2, 4, 4, part).transpose(1, 3, 0, 2, 4)
    inputs_all = lax.all_to_all(inputs.reshape(8, tokens, 4 * part), CZ, 0, 0, tiled=True)
    moments = jnp.stack([first, second]).reshape(2, own, 8, cols).transpose(2, 0, 1, 3)
    moments = lax.all_to_all(moments, CZ, 0, 0, tiled=True)
    moments = stack(moments, "y", True).reshape(4, 2, 4, 2, own, cols)

    basis_low = basis.astype(BF16)
    score_part = jnp.dot(layer_inputs, basis_low, preferred_element_type=F32)
    score_own = scatter_near(score_part, "x")
    score_own = all_sum(score_own, "zh")
    scores = rows_of_x(to_inner(score_own.astype(BF16)))
    scores_all = stack(stack(scores, "zl"), "c").reshape(8 * tokens, rank)

    grad_part = low(scores_all, grads_all.reshape(8 * tokens, cols), TN)
    grad_own = scatter_sum(grad_part, "y")
    grad_low = stack_yz(grad_own.astype(BF16))
    grad_far = shift(grad_low, "c", 1)
    back_part = back_product(place, out_grads, grad_low, grad_far)
    back_own = scatter_near(back_part, "x")
    back_own = all_sum(back_own, "zh")
    backward = rows_of_x(back_own.astype(BF16))
    backward_all = stack(stack(backward, "zl"), "c").reshape(8 * tokens, rank)
    tangent_part = low(inputs_all.reshape(8 * tokens, 4 * part), backward_all, TN)
    tan_near = stack_yz(scatter_sum(tangent_part, "y"), True).reshape(feats // 2, rank)
    tan_far = shift(tan_near, "c", 1)

    tangent, pair = pair_products(place, tan_near, tan_far, basis)
    pair = all_sum(pair, "zh")
    pair = all_sum(pair, "x")
    pairs = stack(stack_yz(pair, True), "c").reshape(32, own, 5 * rank // 2)
    vec, vec_own, rot_own, step, probe_part, scal = finish(
        place, pairs, tangent, basis, layer_inputs
    )
    new_basis = basis + step * vec[:1]
    probe = stack(all_sum(probe_part, "zh"), "x", True).sum(0)[0].astype(BF16)
    along_part = jnp.dot(probe, out_grads, preferred_element_type=F32).reshape(2, 4, cols)
    lead_part = jnp.sum(vec_own * grad_own, axis=0)
    mine = (jnp.arange(2)[:, None] == c) & (jnp.arange(4)[None] == zl)
    push_part = scal[0, 1] * along_part + jnp.where(mine[:, :, None], scal[0, 0] * lead_part, 0.0)
    push_many = jnp.broadcast_to(push_part.transpose(1, 0, 2)[:, None], (4, 4, 2, cols))
    push = lax.all_to_all(push_many.reshape(32, cols), DP, 0, 0, tiled=True).sum(0)

    turned = turn(rot_own, moments)
    grad_new = grad_own + vec_own * push
    moved = jnp.stack(
        [0.9 * turned[0] + 0.1 * grad_new, 0.95 * turned[1] + 0.05 * grad_new * grad_new]
    )
    moved = moved.reshape(2, 8, own, cols).transpose(1, 0, 2, 3)
    moved = lax.all_to_all(moved, CZ, 0, 0, tiled=True)
    moved = moved.transpose(1, 2, 0, 3).reshape(2, own, 8 * cols)
    new_first, new_second = moved[0], moved[1]
    update = new_first / (jnp.sqrt(new_second) + 1e-06)
    return (new_basis, new_first, new_second, update)


def solution(mesh):
    fine = Mesh(mesh.devices.reshape(4, 4, 2, 2, 4), DP + TE)
    return jax.shard_map(
        body,
        mesh=fine,
        in_specs=(P(DP, TE), P(DP, TE), P(TE, None), P(DP, TE), P(DP, TE)),
        out_specs=(P(TE, None), P(DP, TE), P(DP, TE), P(DP, TE)),
        check_vma=False,
    )
```
